32 devices in a mesh: space: 4 (over x, core), tile: 8 (over z, y).
Axes of the slice: x: 2, y: 2, z: 4, core: 2. Of those that a mesh axis runs over, the one named last changes fastest.
Arguments:
- atom_feat: bfloat16 [512, 128, 128], P(('space', 'tile')), may hold values from -6 to 6
- atom_pos: bfloat16 [512, 3, 128], P(('space', 'tile')), may hold values from 0 to 4
- atom_counts: int32 [512], P(('space', 'tile')), may hold values from 32 to 128
- atom_nbrs: int32 [512, 4], P(('space', 'tile')), may hold values from 0 to 511, as said below
- probe_pos: float32 [64, 3, 512], P(('space', 'tile')), may hold values from 0 to 4
- probe_target: float32 [64, 512], P(('space', 'tile')), may hold values from -6 to 6
- tile_blocks: int32 [64, 8], P(('space', 'tile')), may hold values from 0 to 511, as said below
- atom_filter: bfloat16 [128, 1024], replicated, may hold values from -0.5 to 0.5
- probe_filter: bfloat16 [128, 1024], replicated, may hold values from -0.5 to 0.5
- mix_weight: bfloat16 [128, 128], replicated, may hold values from -0.5 to 0.5
- readout: float32 [128], replicated, may hold values from -0.5 to 0.5
Outputs:
- density: float32 [64, 512], P(('space', 'tile'))
- atom_filter_grad: float32 [128, 1024], replicated
- probe_filter_grad: float32 [128, 1024], replicated
- mix_grad: float32 [128, 128], replicated
- readout_grad: float32 [128], replicated
The draws below stay inside these ranges and needn't reach their ends.
Inputs may be any that keep to these rules, and one draw needn't show every extreme that they name: `atom_nbrs`: block g lies on device g // 16 in the order space then tile. The 4 neighbours of a block lie on devices of the same tile index whose space index differs by at most one, cyclically: the first one lower, the second one higher, the third the same; they need not be distinct. `tile_blocks`: the 8 blocks of a tile are distinct and lie on devices of the tile's own space index. The tiles of one device read at most 4 distinct blocks from any one device, and exactly 4 from some device.
All inputs are finite; a program needn't handle non-finite values.
Results may differ from the reference program's by a relative error of at most 0.0061.
Values may be sent and summed in bfloat16 or wider, within the bound.
A program may use at most 64 MiB of HBM per device.

```python
import jax
import jax.numpy as jnp
from jax import lax

C = 128
NRAD = 8
ABLK = 128
PT = 512
KB = 8
KA = 4
BLK_DEV = 16
TL_DEV = 2
RCAP = 4
BLOCKS = 512
TILES = 64
N_SPACE = 4
N_TILE = 8
DEVICES = 32


def draw_atom_nbrs(key, part):
    block_ids = jnp.arange(BLOCKS)
    space_of = block_ids // (N_TILE * BLK_DEV)
    tile_of = block_ids // BLK_DEV % N_TILE
    first_key, second_key = jax.random.split(jax.random.fold_in(key, 11))
    extra = jax.random.randint(first_key, (BLOCKS, KA - 3), -1, 2).astype(jnp.int32)
    shifts = jnp.concatenate([jnp.full((BLOCKS, 1), -1, jnp.int32), jnp.full((BLOCKS, 1), 1, jnp.int32), jnp.zeros((BLOCKS, 1), jnp.int32), extra], axis=1)
    within = jax.random.randint(second_key, (BLOCKS, KA), 0, BLK_DEV).astype(jnp.int32)
    target_space = (space_of[:, None] + shifts + N_SPACE) % N_SPACE
    return ((target_space * N_TILE + tile_of[:, None]) * BLK_DEV + within).astype(jnp.int32)


def draw_tile_blocks(key, part):
    slot_count = TL_DEV * KB
    unit_count = N_TILE * RCAP

    def one_device(device_key, device):
        split_keys = jax.random.split(device_key, 4)
        unit_peer = jnp.arange(unit_count) // RCAP
        favoured = jax.random.randint(split_keys[0], (), 0, N_TILE)
        priority = jax.random.randint(split_keys[1], (unit_count,), 0, 2 ** 20) * unit_count + jnp.arange(unit_count)
        priority = jnp.where(unit_peer == favoured, jnp.arange(unit_count) - unit_count, priority)
        picked = jnp.argsort(priority, stable=True)[:slot_count]
        peer_ids = unit_peer[picked]
        earlier = jnp.tril(jnp.ones((slot_count, slot_count), jnp.int32), -1)
        peer_rank = jnp.sum(earlier * (peer_ids[:, None] == peer_ids[None, :]).astype(jnp.int32), axis=1)
        orders = jax.vmap(lambda peer_key: jax.random.permutation(peer_key, BLK_DEV))(jax.random.split(split_keys[2], N_TILE))
        within = orders[peer_ids, peer_rank]
        region = device // N_TILE
        blocks = (region * N_TILE + peer_ids) * BLK_DEV + within
        shuffled = blocks[jax.random.permutation(split_keys[3], slot_count)]
        return shuffled.reshape(TL_DEV, KB)
    device_keys = jax.random.split(jax.random.fold_in(key, 23), DEVICES)
    return jax.vmap(one_device)(device_keys, jnp.arange(DEVICES)).reshape(TILES, KB).astype(jnp.int32)


def plant(entries, own_key, low, largest):
    shape = entries.shape
    spot = [jax.random.randint(jax.random.fold_in(own_key, axis), (), 0, shape[axis]) for axis in range(len(shape))]
    entries = entries.at[tuple(spot)].set(low)
    longest = shape.index(max(shape))
    spot[longest] = (spot[longest] + 1) % shape[longest]
    return entries.at[tuple(spot)].set(largest)


def level_of(own_key, extent, cuts, least, top_value):
    def one(dim, parts):
        steps = jax.random.uniform(jax.random.fold_in(jax.random.fold_in(own_key, 6), dim), (parts,), jnp.float32, least / len(cuts), top_value / len(cuts))
        return jnp.repeat(jnp.exp(steps), extent[dim] // parts).reshape((-1,) + (1,) * (len(extent) - dim - 1))

    level = one(*cuts[0])
    for cut in cuts[1:]:
        level = level * one(*cut)
    return level


def normal_values(stream_key, dims, deviation, reach, cuts=(), kind=jnp.bfloat16):
    entries = jax.random.normal(stream_key, dims, jnp.float32) * deviation
    if len(cuts) > 0:
        entries = level_of(stream_key, dims, cuts, -0.22, 0.18) * entries
    return jnp.clip(entries, min=-reach, max=reach).astype(kind)


def setup_inputs(seed: int = 0) -> dict:
    key_of = jax.random.split(jax.random.key(seed), 12)
    return {
        "atom_feat": normal_values(key_of[0], (BLOCKS, C, ABLK), 1.0, 6.0, ((0, 32),)),
        "atom_pos": jnp.clip(4.0 * jax.random.uniform(key_of[1], (BLOCKS, 3, ABLK), jnp.float32) ** level_of(key_of[1], (BLOCKS, 3, ABLK), ((0, 32),), -0.2, 0.2), 0.0, 4.0).astype(jnp.bfloat16),
        "atom_counts": plant(jax.random.randint(key_of[2], (BLOCKS,), ABLK // 4, ABLK + 1), jax.random.fold_in(key_of[2], 1), ABLK // 4, ABLK).astype(jnp.int32),
        "atom_nbrs": draw_atom_nbrs(jax.random.fold_in(key_of[11], 71), 0),
        "probe_pos": jnp.clip(4.0 * jax.random.uniform(key_of[4], (TILES, 3, PT), jnp.float32) ** level_of(key_of[4], (TILES, 3, PT), ((0, 32),), -0.2, 0.2), 0.0, 4.0),
        "probe_target": normal_values(key_of[5], (TILES, PT), 1.0, 6.0, ((0, 32),), jnp.float32),
        "tile_blocks": draw_tile_blocks(jax.random.fold_in(key_of[11], 71), 0),
        "atom_filter": normal_values(key_of[7], (C, NRAD * C), C ** -0.5, 0.5),
        "probe_filter": normal_values(key_of[8], (C, NRAD * C), C ** -0.5, 0.5),
        "mix_weight": normal_values(key_of[9], (C, C), C ** -0.5, 0.5),
        "readout": normal_values(key_of[10], (C,), C ** -0.5, 0.5, (), jnp.float32),
    }


CUTOFF = 6.0
SPACING = 0.75
SPREAD = 0.75

def silu_slope(values):
    sigmoid_part = jax.nn.sigmoid(values)
    return sigmoid_part * (1.0 + values * (1.0 - sigmoid_part))

def radial(source, target, factor):
    square = jnp.zeros((source.shape[1], target.shape[1]), source.dtype)
    for component in range(3):
        offset = source[component][:, None] - target[component][None, :]
        square = square + offset * offset
    distance = jnp.sqrt(square + 0.01)
    envelope = jnp.where(distance < CUTOFF, 0.5 * (jnp.cos(jnp.pi * distance / CUTOFF) + 1.0), 0.0)
    centers = jnp.arange(NRAD).astype(source.dtype) * SPACING
    shifted = (distance[None] - centers[:, None, None]) / SPREAD
    return jnp.exp(-shifted * shifted) * (envelope * factor)[None]

def rounded(values):
    narrow = lax.optimization_barrier(values.astype(jnp.bfloat16))
    return narrow.astype(jnp.float32)

def reference(atom_feat, atom_pos, atom_counts, atom_nbrs, probe_pos, probe_target, tile_blocks, atom_filter, probe_filter, mix_weight, readout):
    highest = lax.Precision.HIGHEST
    atom_mask = (jnp.arange(ABLK)[None, :] < atom_counts[:, None]).astype(jnp.float32)
    masked_feat = (atom_feat.astype(jnp.float32) * atom_mask[:, None, :]).astype(jnp.bfloat16)
    coords = atom_pos.astype(jnp.float32)
    atom_scale = (KA * ABLK) ** (-0.5)
    probe_scale = (KB * ABLK) ** (-0.5)

    def atom_block(block_index):
        sources = atom_nbrs[block_index]
        source_feat = masked_feat[sources].astype(jnp.float32)
        target_where = coords[block_index]
        kernel_rows = jax.vmap(lambda source: radial(source, target_where, atom_scale))(coords[sources])
        kernel_rows = rounded(kernel_rows)
        atom_sums = jnp.einsum('kcj,krji->rci', source_feat, kernel_rows)
        atom_sums = atom_sums.astype(jnp.bfloat16).reshape(NRAD * C, ABLK)
        message = jnp.dot(atom_filter, atom_sums, preferred_element_type=jnp.float32)
        updated = ((atom_feat[block_index].astype(jnp.float32) + jax.nn.silu(message)) * atom_mask[block_index][None, :]).astype(jnp.bfloat16)
        return (updated, atom_sums, message)
    updated, atom_sums, message = lax.map(atom_block, jnp.arange(BLOCKS))

    def probe_tile(tile_index):
        read_blocks = tile_blocks[tile_index]
        probe_where = probe_pos[tile_index]

        def kernel_of(block_id):
            return rounded(radial(coords[block_id], probe_where, probe_scale))

        def forward(total_sum, block_id):
            block_term = jnp.einsum('ca,rap->rcp', updated[block_id].astype(jnp.float32), kernel_of(block_id))
            return (total_sum + block_term, None)
        summed, _ = lax.scan(forward, jnp.zeros((NRAD, C, PT), jnp.float32), read_blocks)
        summed = summed.astype(jnp.bfloat16).reshape(NRAD * C, PT)
        hidden = jnp.dot(probe_filter, summed, preferred_element_type=jnp.float32)
        squashed = jax.nn.silu(hidden).astype(jnp.bfloat16)
        mixed_rows = jnp.dot(mix_weight, squashed, preferred_element_type=jnp.float32)
        outer_act = jax.nn.silu(mixed_rows)
        density = jnp.dot(readout, outer_act, precision=highest)
        misfit = (density - probe_target[tile_index]) / PT
        grad_readout = jnp.dot(outer_act, misfit, precision=highest)
        grad_mixed = (readout[:, None] * misfit[None, :] * silu_slope(mixed_rows)).astype(jnp.bfloat16)
        grad_mix = jnp.dot(grad_mixed, squashed.T, preferred_element_type=jnp.float32)
        grad_squashed = jnp.dot(mix_weight.T, grad_mixed, preferred_element_type=jnp.float32)
        grad_hidden = (grad_squashed * silu_slope(hidden)).astype(jnp.bfloat16)
        grad_probe = jnp.dot(grad_hidden, summed.T, preferred_element_type=jnp.float32)
        grad_summed = jnp.dot(probe_filter.T, grad_hidden, preferred_element_type=jnp.float32)
        grad_summed = grad_summed.astype(jnp.bfloat16).astype(jnp.float32).reshape(NRAD, C, PT)

        def backward(block_id):
            return jnp.einsum('rcp,rap->ca', grad_summed, kernel_of(block_id))
        grad_blocks = lax.map(backward, read_blocks)
        return (density, grad_probe, grad_mix, grad_readout, grad_blocks)
    density, grad_probe, grad_mix, grad_readout, grad_blocks = lax.map(probe_tile, jnp.arange(TILES))
    group_count = TILES // TL_DEV
    group_slots = TL_DEV * KB
    group_ids = tile_blocks.reshape(group_count, group_slots)
    group_grads = grad_blocks.reshape(group_count, group_slots, C, ABLK)
    earlier = jnp.tril(jnp.ones((group_slots, group_slots), jnp.float32), -1)

    def group_partial(pair):
        ids_here, grads_here = pair
        same = (ids_here[:, None] == ids_here[None, :]).astype(jnp.float32)
        summed = jnp.einsum('st,tca->sca', same, grads_here, precision=highest)
        repeated = lax.optimization_barrier(jnp.sum(earlier * same, axis=1)) > 0.5
        keep = jnp.where(repeated, 0.0, 1.0).astype(jnp.float32)
        return rounded(summed) * keep[:, None, None]
    partials = lax.map(group_partial, (group_ids, group_grads))
    block_grad = jnp.zeros((BLOCKS, C, ABLK), jnp.float32)
    block_grad = block_grad.at[tile_blocks.reshape(-1)].add(partials.reshape(TILES * KB, C, ABLK))
    grad_message = (block_grad * atom_mask[:, None, :] * silu_slope(message)).astype(jnp.bfloat16)
    atom_filter_grad = jnp.einsum('bca,bda->cd', grad_message.astype(jnp.float32), atom_sums.astype(jnp.float32))
    return (density, atom_filter_grad, lax.optimization_barrier(jnp.sum(grad_probe, axis=0)), lax.optimization_barrier(jnp.sum(grad_mix, axis=0)), lax.optimization_barrier(jnp.sum(grad_readout, axis=0)))
```

```python
import functools
import math

import jax
import jax.numpy as jnp
from jax import lax
from jax.experimental import pallas as pl
from jax.experimental.pallas import tpu as pltpu
from jax.sharding import PartitionSpec as P

CUTOFF = 6.0
SPACING = 0.75
SPREAD = 0.75
LOG2E = 1.4426950408889634
MESH = pl.DeviceIdType.MESH
VMEM_LIMIT = 60 * 1024 * 1024
F32 = jnp.float32
BF16 = jnp.bfloat16


def silu_slope(values):
    s = jax.nn.sigmoid(values)
    return s * (1.0 + values * (1.0 - s))


def scales(filters):
    return [math.exp(-((r * SPACING / SPREAD) ** 2)) for r in range(filters)]


KAPPA = 2.0 * SPACING / SPREAD / SPREAD * LOG2E
BUMP = (0.9999997912905728, -0.23369419608566247, 0.01993802762546961, -0.0008456218103791793)


def radial(square, factor, filters):
    middle = filters // 2
    edge = (CUTOFF * KAPPA) ** 2
    base = [math.sqrt(factor) * c / edge ** (k + 1) for k, c in enumerate(BUMP)]
    reach = square * lax.rsqrt(square)
    up = jnp.exp2(reach)
    down = jnp.exp2(-reach)
    bell = jnp.exp2(square * (-LOG2E / (SPREAD * KAPPA) ** 2) + reach * float(middle))
    wave = ((base[3] * square + base[2]) * square + base[1]) * square + base[0]
    wave = wave * jnp.maximum(edge - square, 0.0)
    values = [None] * filters
    values[middle] = bell * (wave * wave)
    for r in range(middle + 1, filters):
        values[r] = values[r - 1] * up
    for r in range(middle - 1, -1, -1):
        values[r] = values[r + 1] * down
    return values


def square_of(source_cols, target_rows):
    square = None
    for source, target in zip(source_cols, target_rows):
        offset = source - target
        square = offset * offset + 0.01 * KAPPA**2 if square is None else square + offset * offset
    return square


def dot(a, b):
    return jnp.dot(a, b, preferred_element_type=F32)


def dot_nt(a, b):
    return lax.dot_general(a, b, (((1,), (1,)), ((), ())), preferred_element_type=F32)


def atom_radial_kernel(rows_ref, around_where_ref, own_where_ref, radial_ref, columns):
    block = pl.program_id(0)
    width = own_where_ref.shape[2]
    nbrs = radial_ref.shape[1] // width
    filters = radial_ref.shape[2] // width
    factor = (nbrs * width) ** (-0.5)
    own = own_where_ref[0].astype(F32)
    target = [own[c : c + 1, :] * KAPPA for c in range(3)]
    for k in range(nbrs):
        where = around_where_ref[rows_ref[block * nbrs + k]].astype(F32)
        columns[k * width : (k + 1) * width, :] = where[:8].T * KAPPA
    chunk = 32

    def fill(step, carry):
        start = pl.multiple_of(step * chunk, chunk)
        source = [columns[pl.ds(start, chunk), c : c + 1] for c in range(3)]
        for r, value in enumerate(radial(square_of(source, target), factor, filters)):
            radial_ref[0, pl.ds(start, chunk), r * width : (r + 1) * width] = value.astype(BF16)
        return carry

    lax.fori_loop(0, nbrs * width // chunk, fill, 0, unroll=8)


def atom_kernel(
    rows_ref, sides_ref, asked_ref, low_ref, own_ref, high_ref, radial_ref, where_ref, filter_ref,
    sent_ref, sums_ref, message_ref, feats, updated,
):
    block = pl.program_id(0)
    channels, width = own_ref.shape[1:]
    filters = filter_ref.shape[1] // channels
    nbrs = feats.shape[1] // width
    for k in range(nbrs):
        row = rows_ref[block * nbrs + k]
        part = (slice(None), slice(k * width, (k + 1) * width))
        if k < 3:
            feats[part] = (low_ref, high_ref, own_ref)[k][row]
            continue
        side = sides_ref[block * nbrs + k]
        for n, ref in enumerate((low_ref, own_ref, high_ref)):

            @pl.when(side == n)
            def _(ref=ref, row=row, part=part):
                feats[part] = ref[row]

    total = dot(feats[...], radial_ref[0])
    for r, scale in enumerate(scales(filters)):
        part = total[:, r * width : (r + 1) * width] * scale
        sums_ref[0, r * channels : (r + 1) * channels, :] = part.astype(BF16)
    message = dot(filter_ref[...], sums_ref[0])
    message_ref[0] = message
    keep = where_ref[0].astype(F32)[3:4, :]
    fresh = (own_ref[block].astype(F32) + message * jax.nn.sigmoid(message)) * keep
    updated[block] = fresh.astype(BF16)

    @pl.when(block == pl.num_programs(0) - 1)
    def _():
        def pick(slot, carry):
            sent_ref[slot] = updated[asked_ref[slot]]
            return carry

        lax.fori_loop(0, sent_ref.shape[0], pick, 0)


def probe_radial_kernel(source_ref, where_ref, radial_ref, columns):
    width = source_ref.shape[2]
    reads = source_ref.shape[0]
    probes = where_ref.shape[2]
    filters = radial_ref.shape[2] // probes
    factor = (pl.num_programs(1) * reads * width) ** (-0.5)
    for k in range(reads):
        columns[k * width : (k + 1) * width, :] = source_ref[k].T * KAPPA
    chunk, span = 16, 256
    lanes = []
    for p in range(0, probes, span):
        lanes.append([where_ref[0, c : c + 1, p : p + span] * KAPPA for c in range(3)])

    def fill(step, carry):
        start = pl.multiple_of(step * chunk, chunk)
        source = [columns[pl.ds(start, chunk), c : c + 1] for c in range(3)]
        for n, target in enumerate(lanes):
            for r, value in enumerate(radial(square_of(source, target), factor, filters)):
                low = r * probes + n * span
                radial_ref[0, pl.ds(start, chunk), low : low + span] = value.astype(BF16)
        return carry

    lax.fori_loop(0, reads * width // chunk, fill, 0, unroll=4)


def probe_kernel(
    slots_ref, replies_ref, radial_ref, target_ref, filter_ref, mix_ref, readout_ref,
    density_ref, grad_filter_ref, grad_mix_ref, grad_readout_ref, slot_grad_ref,
    feats, summed, turned, slot_total,
):
    tile = pl.program_id(0)
    tiles = pl.num_programs(0)
    channels = mix_ref.shape[0]
    filters = filter_ref.shape[1] // channels
    width = replies_ref.shape[2]
    reads = feats.shape[1] // width
    probes = target_ref.shape[2]

    @pl.when(tile == 0)
    def _():
        slot_total[...] = jnp.zeros_like(slot_total)
        grad_filter_ref[...] = jnp.zeros_like(grad_filter_ref)
        grad_mix_ref[...] = jnp.zeros_like(grad_mix_ref)
        grad_readout_ref[...] = jnp.zeros_like(grad_readout_ref)

    for k in range(reads):
        feats[:, k * width : (k + 1) * width] = replies_ref[slots_ref[tile * reads + k]]
    for r, scale in enumerate(scales(filters)):
        part = dot(feats[...], radial_ref[0, :, r * probes : (r + 1) * probes]) * scale
        summed[r * channels : (r + 1) * channels, :] = (part).astype(BF16)
    hidden = dot(filter_ref[...], summed[...])
    gate = jax.nn.sigmoid(hidden)
    squashed = (hidden * gate).astype(BF16)
    mixed = dot(mix_ref[...], squashed)
    mixed_gate = jax.nn.sigmoid(mixed)
    outer = mixed * mixed_gate
    readout = jnp.broadcast_to(readout_ref[...], (8, channels)).T[:, :1]
    density = jnp.sum(readout * outer, axis=0, keepdims=True)
    density_ref[0] = density
    misfit = (density - target_ref[0]) / probes
    part = jnp.sum(outer * misfit, axis=1, keepdims=True)
    grad_readout_ref[...] += jnp.broadcast_to(part, (channels, channels)).T[:8, :]
    grad_mixed = (
        readout * misfit * (mixed_gate * (1.0 + mixed * (1.0 - mixed_gate)))
    ).astype(BF16)
    grad_mix_ref[...] += dot_nt(grad_mixed, squashed)
    grad_squashed = dot(mix_ref[...].T, grad_mixed)
    grad_hidden = (grad_squashed * (gate * (1.0 + hidden * (1.0 - gate)))).astype(BF16)
    grad_filter_ref[...] += dot_nt(grad_hidden, summed[...])
    grad_sums = dot(grad_hidden.T, filter_ref[...])
    for r, scale in enumerate(scales(filters)):
        part = grad_sums[:, r * channels : (r + 1) * channels] * scale
        turned[r * probes : (r + 1) * probes, :] = part.astype(BF16)
    for k in range(reads):
        slot = slots_ref[tile * reads + k]
        back = dot(radial_ref[0, k * width : (k + 1) * width, :], turned[...])
        slot_total[slot] += back.T

    @pl.when(tile == tiles - 1)
    def _():
        slot_grad_ref[...] = slot_total[...].astype(BF16)


def final_kernel(ids_ref, returned_ref, where_ref, message_ref, sums_ref, grad_ref, totals):
    step = pl.program_id(0)
    group = sums_ref.shape[0]

    @pl.when(step == 0)
    def _():
        totals[...] = jnp.zeros_like(totals)

        def add(slot, carry):
            totals[ids_ref[slot]] += returned_ref[slot].astype(F32)
            return carry

        lax.fori_loop(0, returned_ref.shape[0], add, 0)

    grads = []
    for n in range(group):
        keep = where_ref[n].astype(F32)[3:4, :]
        grad = totals[step * group + n] * keep * silu_slope(message_ref[n])
        grads.append(grad.astype(BF16))
    part = dot_nt(
        jnp.concatenate(grads, axis=1),
        jnp.concatenate([sums_ref[n] for n in range(group)], axis=1),
    )

    @pl.when(step == 0)
    def _():
        grad_ref[...] = part

    @pl.when(step > 0)
    def _():
        grad_ref[...] += part


def reduce_kernel(axes, count, *refs):
    ins, outs = refs[:count], refs[count : 2 * count]
    total, sending, landing, gathered, send_sems, recv_sems = refs[2 * count :]
    rows, lanes = total.shape
    peers = []
    for axis, size in axes:
        here = lax.axis_index(axis)
        peers.append((here, [(here + d) % size for d in range(1, size)]))
    barrier = pltpu.get_barrier_semaphore()
    for (axis, _), (_, others) in zip(axes, peers):
        for other in others:
            pl.semaphore_signal(barrier, inc=1, device_id={axis: other}, device_id_type=MESH)
    pieces = []
    low = 0
    for index, ref in enumerate(ins):
        height = ref.shape[0]
        for left in range(0, ref.shape[1], lanes):
            total[low : low + height, :] = ref[:, left : left + lanes]
            pieces.append((index, left, low, height))
            low += height
    if low < rows:
        total[low:, :] = jnp.zeros((rows - low, lanes), F32)
    pl.semaphore_wait(barrier, sum(size - 1 for _, size in axes))
    sent = []

    def send(source, target, axis, other):
        n = len(sent)
        copy = pltpu.make_async_remote_copy(
            src_ref=source,
            dst_ref=target,
            send_sem=send_sems.at[n],
            recv_sem=recv_sems.at[n],
            device_id={axis: other},
            device_id_type=MESH,
        )
        copy.start()
        sent.append(copy)
        return copy

    start, extent, place, bases = 0, rows, 0, []
    for (axis, size), (here, others) in zip(axes, peers):
        sending[place : place + extent, :] = total[pl.ds(start, extent), :].astype(BF16)
        part = extent // size
        copies = []
        for d, other in enumerate(others):
            copies.append(
                send(
                    sending.at[pl.ds(pl.multiple_of(place + other * part, 16), part)],
                    landing.at[pl.ds(place + d * part, part)],
                    axis,
                    other,
                )
            )
        bases.append((start, extent))
        start = pl.multiple_of(start + here * part, 16)
        for d, copy in enumerate(copies):
            copy.wait_recv()
            total[pl.ds(start, part), :] += landing[
                place + d * part : place + (d + 1) * part, :
            ].astype(F32)
        place += extent
        extent = part
    gathered[pl.ds(start, extent), :] = total[pl.ds(start, extent), :].astype(BF16)
    for n in range(len(axes) - 1, -1, -1):
        axis = axes[n][0]
        mine = gathered.at[pl.ds(start, extent)]
        copies = [send(mine, mine, axis, other) for other in peers[n][1]]
        for copy in copies:
            copy.wait_recv()
        start, extent = bases[n]
    for index, left, low, height in pieces:
        padded = -(-height // 16) * 16
        part = gathered[low : low + padded, :].astype(F32)[:height]
        outs[index][:, left : left + lanes] = part
    for copy in sent:
        copy.wait_send()


def reduce_all(grads, axes, name, collective_id):
    devices = math.prod(size for _, size in axes)
    lanes = grads[0].shape[0]
    real = sum(-(-g.size // (16 * lanes)) * 16 for g in grads)
    rows = -(-real // (16 * devices)) * 16 * devices
    steps = sum(size - 1 for _, size in axes)
    spare = rows + rows // axes[0][1]
    vmem = pl.BlockSpec(memory_space=pltpu.VMEM)
    return pl.pallas_call(
        functools.partial(reduce_kernel, axes, len(grads)),
        in_specs=[vmem] * len(grads),
        out_specs=[vmem] * len(grads),
        out_shape=[jax.ShapeDtypeStruct(g.shape, F32) for g in grads],
        scratch_shapes=[
            pltpu.VMEM((rows, lanes), F32),
            pltpu.VMEM((spare, lanes), BF16),
            pltpu.VMEM((spare, lanes), BF16),
            pltpu.VMEM((rows, lanes), BF16),
            pltpu.SemaphoreType.DMA((2 * steps,)),
            pltpu.SemaphoreType.DMA((2 * steps,)),
        ],
        compiler_params=pltpu.CompilerParams(
            vmem_limit_bytes=VMEM_LIMIT, collective_id=collective_id, has_side_effects=True
        ),
        cost_estimate=cost(20e9),
        name=name,
    )(*grads)


def cost(flops):
    return pl.CostEstimate(flops=int(flops), bytes_accessed=1 << 20, transcendentals=0)


def whole(array):
    return pl.BlockSpec(array.shape, lambda *_: (0,) * array.ndim)


def body(
    atom_feat, atom_pos, atom_counts, atom_nbrs, probe_pos, probe_target, tile_blocks,
    atom_filter, probe_filter, mix_weight, readout,
):
    blocks, channels, width = atom_feat.shape
    tiles, reads = tile_blocks.shape
    probes = probe_pos.shape[2]
    filters = atom_filter.shape[1] // channels
    nbrs = atom_nbrs.shape[1]
    peers = lax.axis_size("tile")
    space_count = lax.axis_size("space")
    here = lax.axis_index("space")
    params = pltpu.CompilerParams(vmem_limit_bytes=VMEM_LIMIT)
    small = params
    mask = (jnp.arange(width)[None, :] < atom_counts[:, None]).astype(BF16)
    where = jnp.concatenate(
        [atom_pos, mask[:, None, :], jnp.zeros((blocks, 12, width), BF16)], axis=1
    )
    forward = [(i, (i + 1) % space_count) for i in range(space_count)]
    backward = [(b, a) for a, b in forward]
    atom_feat = atom_feat * mask[:, None, :]
    low_feat = lax.ppermute(atom_feat, "space", forward)
    high_feat = lax.ppermute(atom_feat, "space", backward)
    around_where = jnp.concatenate(
        [lax.ppermute(where, "space", forward), where, lax.ppermute(where, "space", backward)],
        axis=0,
    )
    sides = ((atom_nbrs // (peers * blocks) - here + 1) % space_count).reshape(-1)
    near_rows = (atom_nbrs % blocks).reshape(-1)

    flat_owner = (tile_blocks // blocks % peers).reshape(-1)
    flat_spot = (tile_blocks % blocks).reshape(-1)
    cap = max(2, 2 * reads * tiles // peers)
    slots = peers * cap
    matches = (flat_owner[:, None, None] == jnp.arange(peers)[None, :, None]) & (
        flat_spot[:, None, None] == jnp.arange(blocks)[None, None, :]
    )
    needed = jnp.any(matches, axis=0).astype(jnp.int32)
    before = jnp.arange(blocks)[:, None] < jnp.arange(blocks)[None, :]
    rank = jnp.sum(needed[:, :, None] * before.astype(jnp.int32)[None], axis=1)
    chosen = (needed[:, None, :] == 1) & (rank[:, None, :] == jnp.arange(cap)[None, :, None])
    request_ids = jnp.sum(chosen.astype(jnp.int32) * jnp.arange(blocks)[None, None, :], axis=2)
    picked_rank = jnp.sum(jnp.where(matches, rank[None], 0), axis=(1, 2))
    slot_index = flat_owner * cap + picked_rank
    flat_where = jnp.broadcast_to(
        atom_pos.reshape(1, blocks * 3, width), (peers, blocks * 3, width)
    )
    asked_row = jnp.pad(request_ids.astype(BF16)[:, None, :], ((0, 0), (0, 15), (0, width - cap)))
    notes = lax.all_to_all(
        jnp.concatenate([flat_where, asked_row], axis=1), "tile",
        split_axis=0, concat_axis=0, tiled=True,
    )
    asked_ids = notes[:, blocks * 3, :cap].astype(jnp.int32).reshape(-1)
    group_where = notes[:, : blocks * 3, :].reshape(peers * blocks, 3, width)

    one = lambda b, *_: (b, 0, 0)
    atom_radial = pl.pallas_call(
        atom_radial_kernel,
        grid_spec=pltpu.PrefetchScalarGridSpec(
            num_scalar_prefetch=1,
            grid=(blocks,),
            in_specs=[whole(around_where), pl.BlockSpec((1, 16, width), one)],
            out_specs=pl.BlockSpec((1, nbrs * width, filters * width), one),
            scratch_shapes=[pltpu.VMEM((nbrs * width, 8), F32)],
        ),
        out_shape=jax.ShapeDtypeStruct((blocks, nbrs * width, filters * width), BF16),
        compiler_params=small,
        cost_estimate=cost(20e9),
        name="atom_radial",
    )(sides * blocks + near_rows, around_where, where)

    sent, sums, message = pl.pallas_call(
        atom_kernel,
        grid_spec=pltpu.PrefetchScalarGridSpec(
            num_scalar_prefetch=3,
            grid=(blocks,),
            in_specs=[
                whole(low_feat),
                whole(atom_feat),
                whole(high_feat),
                pl.BlockSpec((1, nbrs * width, filters * width), one),
                pl.BlockSpec((1, 16, width), one),
                whole(atom_filter),
            ],
            out_specs=[
                pl.BlockSpec((slots, channels, width), lambda *_: (0, 0, 0)),
                pl.BlockSpec((1, filters * channels, width), one),
                pl.BlockSpec((1, channels, width), one),
            ],
            scratch_shapes=[
                pltpu.VMEM((channels, nbrs * width), BF16),
                pltpu.VMEM((blocks, channels, width), BF16),
            ],
        ),
        out_shape=[
            jax.ShapeDtypeStruct((slots, channels, width), BF16),
            jax.ShapeDtypeStruct((blocks, filters * channels, width), BF16),
            jax.ShapeDtypeStruct((blocks, channels, width), F32),
        ],
        compiler_params=small,
        cost_estimate=cost(10e9),
        name="atom_layer",
    )(near_rows, sides, asked_ids, low_feat, atom_feat, high_feat, atom_radial, where, atom_filter)

    sent, group_where = lax.optimization_barrier((sent, group_where))
    replies = lax.all_to_all(
        sent.reshape(peers, cap, channels, width), "tile",
        split_axis=0, concat_axis=0, tiled=True,
    ).reshape(slots, channels, width)

    one_hot = (flat_owner * blocks + flat_spot)[:, None] == jnp.arange(peers * blocks)[None, :]
    source_where = jnp.dot(
        one_hot.astype(BF16), group_where.reshape(peers * blocks, 3 * width),
        preferred_element_type=F32,
    ).reshape(tiles * reads, 3, width)
    source_where = jnp.pad(source_where, ((0, 0), (0, 5), (0, 0)))
    pieces = reads // 2
    per = reads // pieces
    probe_radial = pl.pallas_call(
        probe_radial_kernel,
        grid=(tiles, pieces),
        in_specs=[
            pl.BlockSpec((per, 8, width), lambda t, n: (t * pieces + n, 0, 0)),
            pl.BlockSpec((1, 3, probes), lambda t, n: (t, 0, 0)),
        ],
        out_specs=pl.BlockSpec((1, per * width, filters * probes), lambda t, n: (t, n, 0)),
        scratch_shapes=[pltpu.VMEM((per * width, 8), F32)],
        out_shape=jax.ShapeDtypeStruct((tiles, reads * width, filters * probes), BF16),
        compiler_params=small,
        cost_estimate=cost(20e9),
        name="probe_radial",
    )(source_where, probe_pos)

    readout_row = readout.reshape(1, channels)
    density, grad_filter, grad_mix, grad_readout, slot_grad = pl.pallas_call(
        probe_kernel,
        grid_spec=pltpu.PrefetchScalarGridSpec(
            num_scalar_prefetch=1,
            grid=(tiles,),
            in_specs=[
                whole(replies),
                pl.BlockSpec((1, reads * width, filters * probes), one),
                pl.BlockSpec((1, 1, probes), one),
                whole(probe_filter),
                whole(mix_weight),
                whole(readout_row),
            ],
            out_specs=[
                pl.BlockSpec((1, 1, probes), one),
                pl.BlockSpec((channels, filters * channels), lambda *_: (0, 0)),
                pl.BlockSpec((channels, channels), lambda *_: (0, 0)),
                pl.BlockSpec((8, channels), lambda *_: (0, 0)),
                pl.BlockSpec((slots, channels, width), lambda *_: (0, 0, 0)),
            ],
            scratch_shapes=[
                pltpu.VMEM((channels, reads * width), BF16),
                pltpu.VMEM((filters * channels, probes), BF16),
                pltpu.VMEM((filters * probes, channels), BF16),
                pltpu.VMEM((slots, channels, width), F32),
            ],
        ),
        out_shape=[
            jax.ShapeDtypeStruct((tiles, 1, probes), F32),
            jax.ShapeDtypeStruct((channels, filters * channels), F32),
            jax.ShapeDtypeStruct((channels, channels), F32),
            jax.ShapeDtypeStruct((8, channels), F32),
            jax.ShapeDtypeStruct((slots, channels, width), BF16),
        ],
        compiler_params=params,
        cost_estimate=cost(10e9),
        name="probe_layer",
    )(
        slot_index, replies, probe_radial, probe_target.reshape(tiles, 1, probes),
        probe_filter, mix_weight, readout_row,
    )

    returned = lax.all_to_all(
        slot_grad.reshape(peers, cap, channels, width), "tile",
        split_axis=0, concat_axis=0, tiled=True,
    ).reshape(slots, channels, width)
    axes = (("space", space_count), ("tile", peers))
    group = math.gcd(blocks, 4)
    grad_atom = pl.pallas_call(
        final_kernel,
        grid_spec=pltpu.PrefetchScalarGridSpec(
            num_scalar_prefetch=1,
            grid=(blocks // group,),
            in_specs=[
                whole(returned),
                pl.BlockSpec((group, 16, width), one),
                pl.BlockSpec((group, channels, width), one),
                pl.BlockSpec((group, filters * channels, width), one),
            ],
            out_specs=pl.BlockSpec((channels, filters * channels), lambda *_: (0, 0)),
            scratch_shapes=[pltpu.VMEM((blocks, channels, width), F32)],
        ),
        out_shape=jax.ShapeDtypeStruct((channels, filters * channels), F32),
        compiler_params=params,
        cost_estimate=cost(10e9),
        name="atom_grad",
    )(asked_ids, returned, where, message, sums)
    grad_atom, grad_filter, grad_mix, grad_readout = reduce_all(
        (grad_atom, grad_filter, grad_mix, grad_readout), axes, "grad_reduce", 0
    )
    return (density.reshape(tiles, probes), grad_atom, grad_filter, grad_mix, grad_readout[0])


def solution(mesh):
    return jax.shard_map(
        body,
        mesh=mesh,
        in_specs=(
            P(("space", "tile"), None, None),
            P(("space", "tile"), None, None),
            P(("space", "tile")),
            P(("space", "tile"), None),
            P(("space", "tile"), None, None),
            P(("space", "tile"), None),
            P(("space", "tile"), None),
            P(),
            P(),
            P(),
            P(),
        ),
        out_specs=(P(("space", "tile"), None), P(), P(), P(), P()),
        check_vma=False,
    )
```

```python
import functools
import math

import jax
import jax.numpy as jnp
from jax import lax
from jax.experimental import pallas as pl
from jax.experimental.pallas import tpu as pltpu
from jax.sharding import PartitionSpec as P

CUTOFF = 6.0
SPACING = 0.75
SPREAD = 0.75
LOG2E = 1.4426950408889634
MESH = pl.DeviceIdType.MESH
VMEM_LIMIT = 60 * 1024 * 1024
F32 = jnp.float32
BF16 = jnp.bfloat16
KAPPA = 2.0 * SPACING / SPREAD / SPREAD * LOG2E
BUMP = (0.9999997912905728, -0.23369419608566247, 0.01993802762546961, -0.0008456218103791793)


def silu_slope(values):
    s = jax.nn.sigmoid(values)
    return s * (1.0 + values * (1.0 - s))


def dot(a, b):
    return jnp.dot(a, b, preferred_element_type=F32)


def dot_nt(a, b):
    return lax.dot_general(a, b, (((1,), (1,)), ((), ())), preferred_element_type=F32)


def dot_tn(a, b):
    return lax.dot_general(a, b, (((0,), (0,)), ((), ())), preferred_element_type=F32)


def radial(square, factor, filters):
    middle = filters // 2
    step = SPACING / SPREAD
    edge = (CUTOFF * KAPPA) ** 2
    base = [
        math.sqrt(factor) * math.exp(-0.5 * (middle * step) ** 2) * c / edge ** (k + 1)
        for k, c in enumerate(BUMP)
    ]
    reach = square * lax.rsqrt(square)
    up = jnp.exp2(reach - (2 * middle + 1) * step * step * LOG2E)
    down = jnp.exp2((2 * middle - 1) * step * step * LOG2E - reach)
    bell = jnp.exp2(square * (-LOG2E / (SPREAD * KAPPA) ** 2) + reach * float(middle))
    wave = ((base[3] * square + base[2]) * square + base[1]) * square + base[0]
    wave = wave * jnp.maximum(edge - square, 0.0)
    values = [None] * filters
    values[middle] = bell * (wave * wave)
    for r in range(middle + 1, filters):
        k = r - middle - 1
        values[r] = values[r - 1] * (up if k == 0 else up * math.exp(-2.0 * k * step * step))
    for r in range(middle - 1, -1, -1):
        k = middle - 1 - r
        values[r] = values[r + 1] * (down if k == 0 else down * math.exp(-2.0 * k * step * step))
    return values


def thirds(values):
    out = []
    for _ in range(3):
        part = values.astype(BF16).astype(F32)
        out.append(part)
        values = values - part
    return out


def source_rows(where):
    x = [where[c : c + 1] for c in range(3)]
    norm = thirds(KAPPA**2 * (x[0] * x[0] + x[1] * x[1] + x[2] * x[2]))
    one = jnp.ones_like(x[0])
    return jnp.concatenate(x * 3 + norm + [one] * 3 + [one * 0.0], axis=0).astype(BF16)


def target_rows(where):
    y = [where[c : c + 1] for c in range(3)]
    norm = thirds(KAPPA**2 * (y[0] * y[0] + y[1] * y[1] + y[2] * y[2] + 0.01))
    y = [thirds(-2.0 * KAPPA**2 * part) for part in y]
    one = jnp.ones_like(norm[0])
    rows = [y[c][k] for k in range(3) for c in range(3)] + [one] * 3 + norm + [one * 0.0]
    return jnp.concatenate(rows, axis=0).astype(BF16)


def slot_tables(rows, me, peers, cap, blocks, reads):
    lanes = rows.shape[1]
    cols = rows.T
    row = lambda n: rows[n : n + 1, :]
    col = lambda n: cols[:, n : n + 1]
    block, owner, asker, tile, place = range(5)
    down = lax.broadcasted_iota(jnp.int32, (lanes, lanes), 0)
    along = lax.broadcasted_iota(jnp.int32, (lanes, lanes), 1)
    lane = along.astype(F32)
    yes = lambda cond: jnp.where(cond, 1.0, 0.0)
    same = yes(col(asker) == row(asker))
    equal = same * yes(col(block) == row(block))
    first_row = yes(jnp.sum(equal * yes(down < along), axis=0, keepdims=True) < 0.5)
    first_col = yes(jnp.sum(equal * yes(along < down), axis=1, keepdims=True) < 0.5)
    group = same * yes(col(owner) == row(owner))
    rank_col = jnp.sum(group * yes(row(block) < col(block)) * first_row, axis=1, keepdims=True)
    rank_row = jnp.sum(group * yes(col(block) < row(block)) * first_col, axis=0, keepdims=True)
    spot = col(block) - me * float(blocks)
    mine = yes(col(owner) == me) * first_col
    put = lambda cond, value: jnp.sum(yes(cond) * value, axis=0, keepdims=True)
    asked = put(col(asker) * cap + rank_col == lane, mine * spot)
    slot = row(owner) * cap + rank_row
    arrival = put(col(asker) * blocks + spot == lane, mine * (rank_col + 1.0))
    slot_col = col(owner) * cap + rank_col
    own = yes(col(asker) == me)
    fill = put(col(tile) * (peers * cap) + slot_col == lane, own * (col(place) + 1.0))
    limit = lambda value, most: jnp.clip(value, 0.0, float(most))
    rows = [
        limit(asked, blocks - 1), limit(slot, peers * cap - 1), limit(arrival, cap), limit(fill, reads),
        jnp.zeros((4, lanes), F32),
    ]
    return jnp.concatenate(rows, axis=0).astype(jnp.int32)


def within(value, most):
    return jnp.minimum(jnp.maximum(value, 0), most)


def send(source, target, send_sem, recv_sem, device):
    copy = pltpu.make_async_remote_copy(
        src_ref=source, dst_ref=target, send_sem=send_sem, recv_sem=recv_sem,
        device_id=device, device_id_type=MESH,
    )
    copy.start()
    return copy


def reduce(groups, total, sending, landing, gathered, send_sems, recv_sems):
    rows = total.shape[0]
    sent = []

    def go(source, target, device):
        n = len(sent)
        sent.append(send(source, target, send_sems.at[n], recv_sems.at[n], device))
        return sent[-1]

    start, extent, place, bases = 0, rows, 0, []
    for size, here, others in groups:
        sending[place : place + extent, :] = total[pl.ds(start, extent), :].astype(BF16)
        part = extent // size
        copies = []
        for d, (index, device) in enumerate(others):
            source = sending.at[pl.ds(pl.multiple_of(place + index * part, 16), part)]
            copies.append(go(source, landing.at[pl.ds(place + d * part, part)], device))
        bases.append((start, extent))
        start = pl.multiple_of(start + here * part, 16)
        for copy in copies:
            copy.wait_recv()
        add = total[pl.ds(start, part), :]
        for d in range(len(others)):
            add = add + landing[place + d * part : place + (d + 1) * part, :].astype(F32)
        total[pl.ds(start, part), :] = add
        place += extent
        extent = part
    gathered[pl.ds(start, extent), :] = total[pl.ds(start, extent), :].astype(BF16)
    for n in range(len(groups) - 1, -1, -1):
        mine = gathered.at[pl.ds(start, extent)]
        copies = [go(mine, mine, device) for _, device in groups[n][2]]
        for copy in copies:
            copy.wait_recv()
        start, extent = bases[n]
    return sent


def step_kernel(
    space_count, peers, cap,
    near_ref, feat_ref, where_ref, notes_ref, want_ref, probe_ref, target_ref, atom_filter_ref, probe_filter_ref,
    mix_ref, readout_ref,
    density_ref, probe_sum_ref, atom_sum_ref,
    around, places, region, notes, sources, targets, square, atom_rad, sums, message, updated, table, index,
    sent, replies, read_where, wide, probe_rad, summed, grads, backs, sent_back, returned, messages_grad,
    probe_total, probe_sending, probe_landing, atom_total, atom_sending, atom_landing,
    near_sems, tile_sems, reply_sems, return_sems, probe_sems, atom_sems, table_sem,
):
    blocks, channels, width = feat_ref.shape
    tiles, _, probes = probe_ref.shape
    filters = atom_filter_ref.shape[1] // channels
    nbrs = near_ref.shape[0] // blocks
    reads = want_ref.shape[0] // 8 // tiles
    slots = peers * cap
    s, t = lax.axis_index("space"), lax.axis_index("tile")
    low, high = (s + space_count - 1) % space_count, (s + 1) % space_count
    core = s % 2
    sibling = s - core + (1 - core)
    chips = space_count // 2
    row = s // 2
    hops = sorted(range(1, peers), key=lambda d: -min(d, peers - d))
    tile_peers = [(t + d) % peers for d in hops]
    row_peers = [(row + d) % chips for d in range(1, chips)]
    pair_group = (2, core, [(1 - core, {"space": sibling})])
    row_group = (chips, row, [(r, {"space": r * 2 + core}) for r in row_peers])
    tile_group = (peers, t, [(p, {"tile": p}) for p in tile_peers])
    chip_list = []
    for a in range(chips):
        for b in range(peers):
            if a or b:
                r, p = (row + a) % chips, (t + b) % peers
                chip_list.append((r * peers + p, {"space": r * 2 + core, "tile": p}))
    chip_group = (chips * peers, row * peers + t, chip_list)

    barrier = pltpu.get_barrier_semaphore()
    greeted = [{"space": low}, {"space": high}, {"space": sibling}] + [d for _, d in chip_list]
    for device in greeted:
        pl.semaphore_signal(barrier, inc=1, device_id=device, device_id_type=MESH)
    for b in range(blocks):
        keep = where_ref[4 * b + 3 : 4 * b + 4, :]
        around[blocks + b] = feat_ref[b] * keep
    region[pl.ds(pl.multiple_of(t * 4 * blocks, 16), 4 * blocks), :] = where_ref[...]
    notes[t] = notes_ref[...]
    pl.semaphore_wait(barrier, len(greeted))

    place_copies = [
        send(where_ref, places.at[1], near_sems.at[0, 0], near_sems.at[1, 0], {"space": low}),
        send(where_ref, places.at[0], near_sems.at[0, 1], near_sems.at[1, 1], {"space": high}),
    ]
    feat_copies = [
        send(
            around.at[pl.ds(blocks, blocks)], around.at[pl.ds(2 * blocks, blocks)],
            near_sems.at[0, 2], near_sems.at[1, 2], {"space": low},
        ),
        send(
            around.at[pl.ds(blocks, blocks)], around.at[pl.ds(0, blocks)],
            near_sems.at[0, 3], near_sems.at[1, 3], {"space": high},
        ),
    ]
    tile_copies = []
    for d, p in enumerate(tile_peers):
        mine = pl.ds(pl.multiple_of(t * 4 * blocks, 16), 4 * blocks)
        tile_copies.append(
            send(notes_ref, notes.at[t], tile_sems.at[0, 2 * d], tile_sems.at[1, 2 * d], {"tile": p})
        )
        tile_copies.append(
            send(where_ref, region.at[mine], tile_sems.at[0, 2 * d + 1], tile_sems.at[1, 2 * d + 1], {"tile": p})
        )

    for b in range(blocks):
        where = where_ref[4 * b : 4 * b + 4, :].astype(F32)
        sources[blocks + b] = source_rows(where)
        targets[b] = target_rows(where)
    for copy in place_copies:
        copy.wait_recv()
    for side in range(2):
        for b in range(blocks):
            where = places[side, 4 * b : 4 * b + 4, :].astype(F32)
            sources[2 * blocks * side + b] = source_rows(where)

    factor = (nbrs * width) ** (-0.5)
    chunk = 32

    def atom_radial(b, carry):
        near = [sources[near_ref[b * nbrs + k]] for k in range(nbrs)]
        square[...] = dot_tn(jnp.concatenate(near, axis=1), targets[b])

        def fill(step, carry):
            at = pl.ds(pl.multiple_of(step * chunk, chunk), chunk)
            for r, value in enumerate(radial(square[at, :], factor, filters)):
                atom_rad[b, at, r * width : (r + 1) * width] = value.astype(BF16)
            return carry

        return lax.fori_loop(0, nbrs * width // chunk, fill, carry, unroll=8)

    lax.fori_loop(0, blocks, atom_radial, 0)

    for copy in tile_copies:
        copy.wait_recv()
    rows = notes[0]
    for p in range(1, peers):
        rows = rows + notes[p]
    table[...] = slot_tables(rows.astype(F32), t.astype(F32), peers, cap, blocks, reads)
    to_scalars = pltpu.make_async_copy(table, index, table_sem)
    to_scalars.start()
    to_scalars.wait()
    lane = lax.broadcasted_iota(jnp.int32, (want_ref.shape[0], region.shape[0]), 1)
    pick = jnp.where(want_ref[:, :1] == lane, 1.0, 0.0).astype(BF16)
    read_where[...] = dot(pick, region[...])

    for copy in feat_copies:
        copy.wait_recv()

    def atom_layer(b, carry):
        feats = jnp.concatenate([around[near_ref[b * nbrs + k]] for k in range(nbrs)], axis=1)
        at = pl.ds(pl.multiple_of(b * width, width), width)
        for r in range(0, filters, 2):
            part = dot(feats, atom_rad[b, :, r * width : (r + 2) * width])
            sums[r * channels : (r + 1) * channels, at] = part[:, :width].astype(BF16)
            sums[(r + 1) * channels : (r + 2) * channels, at] = part[:, width:].astype(BF16)
        out = dot(atom_filter_ref[...], sums[:, at])
        message[b] = out
        own = around[blocks + b].astype(F32)
        keep = message_mask(b)
        updated[b] = (own + out * jax.nn.sigmoid(out) * keep).astype(BF16)
        return carry

    def message_mask(b):
        return messages_grad[b][3:4, :]

    for b in range(blocks):
        messages_grad[b] = jnp.concatenate(
            [where_ref[4 * b : 4 * b + 4, :].astype(F32), jnp.zeros((4, width), F32)], axis=0
        )
    lax.fori_loop(0, blocks, atom_layer, 0, unroll=2)

    for slot in range(slots):
        sent[slot] = updated[within(index[0, slot], blocks - 1)]
    mine = pl.ds(t * cap, cap)
    reply_copies = []
    for d, p in enumerate(tile_peers):
        reply_copies.append(
            send(sent.at[pl.ds(p * cap, cap)], replies.at[mine], reply_sems.at[0, d], reply_sems.at[1, d], {"tile": p})
        )
    replies[mine] = sent[mine]
    probe_factor = (reads * width) ** (-0.5)
    span = min(256, probes)
    for tile in range(tiles):
        near = [
            source_rows(read_where[(tile * reads + k) * 8 : (tile * reads + k + 1) * 8, :]) for k in range(reads)
        ]
        wide[...] = dot_tn(jnp.concatenate(near, axis=1), target_rows(probe_ref[tile]))

        def fill(step, carry, tile=tile):
            at = pl.ds(pl.multiple_of(step * 16, 16), 16)
            for p in range(0, probes, span):
                for r, value in enumerate(radial(wide[at, p : p + span], probe_factor, filters)):
                    probe_rad[tile, at, r * probes + p : r * probes + p + span] = value.astype(BF16)
            return carry

        lax.fori_loop(0, reads * width // 16, fill, 0, unroll=4)
    for copy in reply_copies:
        copy.wait_recv()

    readout = jnp.broadcast_to(readout_ref[...], (8, channels)).T[:, :1]
    backs[0] = jnp.zeros_like(backs[0])
    grad_filter = grad_mix = grad_readout = None
    for tile in range(tiles):
        feats = jnp.concatenate(
            [replies[within(index[1, (t * tiles + tile) * reads + k], slots - 1)] for k in range(reads)], axis=1
        )

        def forward(r, carry, tile=tile, feats=feats):
            at = pl.ds(pl.multiple_of(r * probes, probes), probes)
            part = dot(feats, probe_rad[tile, :, at])
            summed[tile, pl.ds(pl.multiple_of(r * channels, channels), channels), :] = part.astype(BF16)
            return carry

        lax.fori_loop(0, filters, forward, 0)
        hidden = dot(probe_filter_ref[...], summed[tile])
        gate = jax.nn.sigmoid(hidden)
        squashed = (hidden * gate).astype(BF16)
        mixed = dot(mix_ref[...], squashed)
        mixed_gate = jax.nn.sigmoid(mixed)
        outer = mixed * mixed_gate
        density = jnp.sum(readout * outer, axis=0, keepdims=True)
        density_ref[tile : tile + 1, :] = density
        misfit = (density - target_ref[tile : tile + 1, :]) / probes
        part = jnp.sum(outer * misfit, axis=1, keepdims=True)
        part = jnp.broadcast_to(part, (channels, channels)).T[:16, :]
        grad_readout = part if grad_readout is None else grad_readout + part
        grad_mixed = (readout * misfit * (mixed_gate * (1.0 + mixed * (1.0 - mixed_gate)))).astype(BF16)
        part = dot_nt(grad_mixed, squashed)
        grad_mix = part if grad_mix is None else grad_mix + part
        grad_squashed = dot_tn(mix_ref[...], grad_mixed)
        grad_hidden = (grad_squashed * (gate * (1.0 + hidden * (1.0 - gate)))).astype(BF16)
        part = dot_nt(grad_hidden, summed[tile])
        for r in range(filters):
            at = slice(r * channels, (r + 1) * channels)
            piece = part[:, at]
            probe_total[at, :] = piece if tile == 0 else probe_total[at, :] + piece
        for r in range(filters):
            piece = dot_tn(probe_filter_ref[:, r * channels : (r + 1) * channels], grad_hidden)
            grads[:, r * probes : (r + 1) * probes] = piece.astype(BF16)
        for k in range(0, reads, 2):
            back = dot_nt(grads[...], probe_rad[tile, k * width : (k + 2) * width, :])
            for n in range(2):
                backs[1 + tile * reads + k + n] = back[:, n * width : (n + 1) * width]
    base = filters * channels
    probe_total[base : base + channels, :] = grad_mix
    probe_total[base + channels : base + channels + 16, :] = grad_readout
    spare = probe_total.shape[0] - base - channels - 16
    if spare:
        probe_total[base + channels + 16 :, :] = jnp.zeros((spare, channels), F32)

    for slot in range(slots):
        total = backs[within(index[3, slot], reads)]
        for tile in range(1, tiles):
            place = within(index[3, tile * slots + slot], reads)
            total = total + backs[jnp.where(place > 0, place + tile * reads, 0)]
        sent_back[slot] = total.astype(BF16)
    step = cap + 1
    landing = pl.ds(t * step + 1, cap)
    return_copies = []
    for d, p in enumerate(tile_peers):
        return_copies.append(
            send(
                sent_back.at[pl.ds(p * cap, cap)], returned.at[landing],
                return_sems.at[0, d], return_sems.at[1, d], {"tile": p},
            )
        )
    for p in range(peers):
        returned[p * step] = jnp.zeros((channels, width), BF16)
    returned[landing] = sent_back[mine]
    probe_copies = reduce(
        [pair_group, row_group, tile_group], probe_total, probe_sending, probe_landing, probe_sum_ref,
        probe_sems.at[0], probe_sems.at[1],
    )
    for copy in return_copies:
        copy.wait_recv()

    def atom_grad(b, carry):
        total = None
        for p in range(peers):
            part = returned[p * step + within(index[2, p * blocks + b], cap)].astype(F32)
            total = part if total is None else total + part
        grad = total * message_mask(b) * silu_slope(message[b])
        grads[:, pl.ds(pl.multiple_of(b * width, width), width)] = grad.astype(BF16)
        return carry

    lax.fori_loop(0, blocks, atom_grad, 0, unroll=2)
    for r in range(0, filters, 2):
        part = dot_nt(grads[:, : blocks * width], sums[r * channels : (r + 2) * channels, :])
        for n in range(2):
            at = slice((r + n) * channels, (r + n + 1) * channels)
            atom_total[at, :] = part[:, n * channels : (n + 1) * channels]
    spare = atom_total.shape[0] - base
    if spare:
        atom_total[base:, :] = jnp.zeros((spare, channels), F32)
    atom_copies = reduce(
        [pair_group, chip_group], atom_total, atom_sending, atom_landing, atom_sum_ref,
        atom_sems.at[0], atom_sems.at[1],
    )
    every = place_copies + feat_copies + tile_copies + reply_copies + return_copies + probe_copies + atom_copies
    for copy in every:
        copy.wait_send()


def unpack_kernel(density_ref, probe_ref, atom_ref, out_ref, grad_atom_ref, grad_probe_ref, grad_mix_ref, readout_ref):
    channels = grad_mix_ref.shape[0]
    filters = grad_atom_ref.shape[1] // channels
    out_ref[...] = density_ref[...]
    for r in range(filters):
        at = slice(r * channels, (r + 1) * channels)
        grad_atom_ref[:, at] = atom_ref[at, :].astype(F32)
        grad_probe_ref[:, at] = probe_ref[at, :].astype(F32)
    base = filters * channels
    grad_mix_ref[...] = probe_ref[base : base + channels, :].astype(F32)
    readout_ref[...] = probe_ref[base + channels : base + channels + 16, :].astype(F32)[:1]


def body(
    atom_feat, atom_pos, atom_counts, atom_nbrs, probe_pos, probe_target, tile_blocks,
    atom_filter, probe_filter, mix_weight, readout,
):
    blocks, channels, width = atom_feat.shape
    tiles, reads = tile_blocks.shape
    probes = probe_pos.shape[2]
    filters = atom_filter.shape[1] // channels
    nbrs = atom_nbrs.shape[1]
    peers = lax.axis_size("tile")
    space_count = lax.axis_size("space")
    devices = peers * space_count
    here, mine = lax.axis_index("space"), lax.axis_index("tile")
    cap = max(2, 2 * reads * tiles // peers)
    slots = peers * cap
    own = tiles * reads
    mask = (jnp.arange(width)[None, :] < atom_counts[:, None]).astype(BF16)
    where = jnp.concatenate([atom_pos, mask[:, None, :]], axis=1).reshape(blocks * 4, width)
    sides = (atom_nbrs // (peers * blocks) - here + 1) % space_count
    near = (sides * blocks + atom_nbrs % blocks).reshape(-1)
    lanes = max(peers * own, peers * blocks, tiles * slots)
    flat = (tile_blocks % (peers * blocks)).reshape(-1)
    ask = jnp.arange(own)
    note = jnp.stack(
        [flat, flat // blocks, jnp.full((own,), mine, jnp.int32), ask // reads, ask % reads, ask * 0, ask * 0, ask * 0]
    ).astype(jnp.int32)
    held = jnp.arange(lanes)[None, :] // own == mine
    note = jnp.where(held, jnp.tile(note, (1, lanes // own)), 0)
    part = jnp.arange(8)[None, :]
    want = jnp.where(part < 4, flat[:, None] * 4 + part, -1).reshape(own * 8, 1)
    want = jnp.broadcast_to(want, (own * 8, 128)).astype(jnp.int32)

    unit = 16 * devices
    atom_rows = -(-filters * channels // unit) * unit
    probe_rows = -(-(filters * channels + channels + 16) // unit) * unit
    vmem = pl.BlockSpec(memory_space=pltpu.VMEM)
    smem = pl.BlockSpec(memory_space=pltpu.SMEM)
    dma = pltpu.SemaphoreType.DMA
    chips = space_count // 2
    probe_space = probe_rows + probe_rows // 2 + probe_rows // (2 * chips)
    density, probe_sum, atom_sum = pl.pallas_call(
        functools.partial(step_kernel, space_count, peers, cap),
        in_specs=[smem] + [vmem] * 10,
        out_specs=[vmem] * 3,
        out_shape=[
            jax.ShapeDtypeStruct((tiles, probes), F32),
            jax.ShapeDtypeStruct((probe_rows, channels), BF16),
            jax.ShapeDtypeStruct((atom_rows, channels), BF16),
        ],
        scratch_shapes=[
            pltpu.VMEM((3 * blocks, channels, width), BF16),
            pltpu.VMEM((2, 4 * blocks, width), BF16),
            pltpu.VMEM((peers * 4 * blocks, width), BF16),
            pltpu.VMEM((peers, 8, lanes), jnp.int32),
            pltpu.VMEM((3 * blocks, 16, width), BF16),
            pltpu.VMEM((blocks, 16, width), BF16),
            pltpu.VMEM((nbrs * width, width), F32),
            pltpu.VMEM((blocks, nbrs * width, filters * width), BF16),
            pltpu.VMEM((filters * channels, blocks * width), BF16),
            pltpu.VMEM((blocks, channels, width), F32),
            pltpu.VMEM((blocks, channels, width), BF16),
            pltpu.VMEM((8, lanes), jnp.int32),
            pltpu.SMEM((8, lanes), jnp.int32),
            pltpu.VMEM((slots, channels, width), BF16),
            pltpu.VMEM((slots, channels, width), BF16),
            pltpu.VMEM((own * 8, width), F32),
            pltpu.VMEM((reads * width, probes), F32),
            pltpu.VMEM((tiles, reads * width, filters * probes), BF16),
            pltpu.VMEM((tiles, filters * channels, probes), BF16),
            pltpu.VMEM((channels, max(filters * probes, blocks * width)), BF16),
            pltpu.VMEM((1 + own, channels, width), F32),
            pltpu.VMEM((slots, channels, width), BF16),
            pltpu.VMEM((peers * (cap + 1), channels, width), BF16),
            pltpu.VMEM((blocks, 8, width), F32),
            pltpu.VMEM((probe_rows, channels), F32),
            pltpu.VMEM((probe_space, channels), BF16),
            pltpu.VMEM((probe_space, channels), BF16),
            pltpu.VMEM((atom_rows, channels), F32),
            pltpu.VMEM((atom_rows + atom_rows // 2, channels), BF16),
            pltpu.VMEM((atom_rows + atom_rows // 2, channels), BF16),
            dma((2, 4)),
            dma((2, 2 * (peers - 1))),
            dma((2, peers - 1)),
            dma((2, peers - 1)),
            dma((2, 2 * (1 + chips - 1 + peers - 1))),
            dma((2, 2 * (1 + chips * peers - 1))),
            dma,
        ],
        compiler_params=pltpu.CompilerParams(
            vmem_limit_bytes=VMEM_LIMIT, collective_id=0, has_side_effects=True
        ),
        name="network_step",
    )(
        near, atom_feat, where, note, want, probe_pos, probe_target, atom_filter, probe_filter, mix_weight,
        readout.reshape(1, channels),
    )
    density, grad_atom, grad_probe, grad_mix, grad_readout = pl.pallas_call(
        unpack_kernel,
        in_specs=[vmem] * 3,
        out_specs=[vmem] * 5,
        out_shape=[
            jax.ShapeDtypeStruct((tiles, probes), F32),
            jax.ShapeDtypeStruct((channels, filters * channels), F32),
            jax.ShapeDtypeStruct((channels, filters * channels), F32),
            jax.ShapeDtypeStruct((channels, channels), F32),
            jax.ShapeDtypeStruct((1, channels), F32),
        ],
        name="unpack",
    )(density, probe_sum, atom_sum)
    return density, grad_atom, grad_probe, grad_mix, grad_readout.reshape(channels)


def solution(mesh):
    return jax.shard_map(
        body,
        mesh=mesh,
        in_specs=(
            P(("space", "tile"), None, None),
            P(("space", "tile"), None, None),
            P(("space", "tile")),
            P(("space", "tile"), None),
            P(("space", "tile"), None, None),
            P(("space", "tile"), None),
            P(("space", "tile"), None),
            P(),
            P(),
            P(),
            P(),
        ),
        out_specs=(P(("space", "tile"), None), P(), P(), P(), P()),
        check_vma=False,
    )
```

```python
import functools
import math

import jax
import jax.numpy as jnp
from jax import lax
from jax.experimental import pallas as pl
from jax.experimental.pallas import tpu as pltpu
from jax.sharding import PartitionSpec as P

CUTOFF = 6.0
SPACING = 0.75
SPREAD = 0.75
LOG2E = 1.4426950408889634
MESH = pl.DeviceIdType.MESH
VMEM_LIMIT = 60 * 1024 * 1024
F32 = jnp.float32
BF16 = jnp.bfloat16
KAPPA = 2.0 * SPACING / SPREAD / SPREAD * LOG2E
BUMP = (0.9999997912905728, -0.23369419608566247, 0.01993802762546961, -0.0008456218103791793)


def silu_slope(values):
    s = jax.nn.sigmoid(values)
    return s * (1.0 + values * (1.0 - s))


def dot(a, b):
    return jnp.dot(a, b, preferred_element_type=F32)


def dot_nt(a, b):
    return lax.dot_general(a, b, (((1,), (1,)), ((), ())), preferred_element_type=F32)


def dot_tn(a, b):
    return lax.dot_general(a, b, (((0,), (0,)), ((), ())), preferred_element_type=F32)


def radial(square, factor, filters):
    middle = filters // 2
    step = SPACING / SPREAD
    edge = (CUTOFF * KAPPA) ** 2
    base = [
        math.sqrt(factor) * math.exp(-0.5 * (middle * step) ** 2) * c / edge ** (k + 1)
        for k, c in enumerate(BUMP)
    ]
    reach = square * lax.rsqrt(square)
    up = jnp.exp2(reach - (2 * middle + 1) * step * step * LOG2E)
    down = jnp.exp2((2 * middle - 1) * step * step * LOG2E - reach)
    bell = jnp.exp2(square * (-LOG2E / (SPREAD * KAPPA) ** 2) + reach * float(middle))
    wave = ((base[3] * square + base[2]) * square + base[1]) * square + base[0]
    wave = wave * jnp.maximum(edge - square, 0.0)
    values = [None] * filters
    values[middle] = bell * (wave * wave)
    for r in range(middle + 1, filters):
        k = r - middle - 1
        values[r] = values[r - 1] * (up if k == 0 else up * math.exp(-2.0 * k * step * step))
    for r in range(middle - 1, -1, -1):
        k = middle - 1 - r
        values[r] = values[r + 1] * (down if k == 0 else down * math.exp(-2.0 * k * step * step))
    return values


def thirds(values):
    out = []
    for _ in range(3):
        part = values.astype(BF16).astype(F32)
        out.append(part)
        values = values - part
    return out


def source_rows(where):
    x = [where[c : c + 1] for c in range(3)]
    norm = thirds(KAPPA**2 * (x[0] * x[0] + x[1] * x[1] + x[2] * x[2]))
    one = jnp.ones_like(x[0])
    return jnp.concatenate(x * 3 + norm + [one] * 3 + [one * 0.0], axis=0).astype(BF16)


def target_rows(where):
    y = [where[c : c + 1] for c in range(3)]
    norm = thirds(KAPPA**2 * (y[0] * y[0] + y[1] * y[1] + y[2] * y[2] + 0.01))
    y = [thirds(-2.0 * KAPPA**2 * part) for part in y]
    one = jnp.ones_like(norm[0])
    rows = [y[c][k] for k in range(3) for c in range(3)] + [one] * 3 + norm + [one * 0.0]
    return jnp.concatenate(rows, axis=0).astype(BF16)


def slot_tables(rows, me, peers, cap, blocks, reads):
    lanes = rows.shape[1]
    cols = rows.T
    row = lambda n: rows[n : n + 1, :]
    col = lambda n: cols[:, n : n + 1]
    block, owner, asker, tile, place = range(5)
    down = lax.broadcasted_iota(jnp.int32, (lanes, lanes), 0)
    along = lax.broadcasted_iota(jnp.int32, (lanes, lanes), 1)
    lane = along.astype(F32)
    yes = lambda cond: jnp.where(cond, 1.0, 0.0)
    same = yes(col(asker) == row(asker))
    equal = same * yes(col(block) == row(block))
    first_row = yes(jnp.sum(equal * yes(down < along), axis=0, keepdims=True) < 0.5)
    first_col = yes(jnp.sum(equal * yes(along < down), axis=1, keepdims=True) < 0.5)
    group = same * yes(col(owner) == row(owner))
    rank_col = jnp.sum(group * yes(row(block) < col(block)) * first_row, axis=1, keepdims=True)
    rank_row = jnp.sum(group * yes(col(block) < row(block)) * first_col, axis=0, keepdims=True)
    spot = col(block) - me * float(blocks)
    mine = yes(col(owner) == me) * first_col
    put = lambda cond, value: jnp.sum(yes(cond) * value, axis=0, keepdims=True)
    asked = put(col(asker) * cap + rank_col == lane, mine * spot)
    slot = row(owner) * cap + rank_row
    arrival = put(col(asker) * blocks + spot == lane, mine * (rank_col + 1.0))
    slot_col = col(owner) * cap + rank_col
    own = yes(col(asker) == me)
    fill = put(col(tile) * (peers * cap) + slot_col == lane, own * (col(place) + 1.0))
    limit = lambda value, most: jnp.clip(value, 0.0, float(most))
    rows = [
        limit(asked, blocks - 1), limit(slot, peers * cap - 1), limit(arrival, cap), limit(fill, reads),
        jnp.zeros((4, lanes), F32),
    ]
    return jnp.concatenate(rows, axis=0).astype(jnp.int32)


def within(value, most):
    return jnp.minimum(jnp.maximum(value, 0), most)


def send(source, target, send_sem, recv_sem, device):
    copy = pltpu.make_async_remote_copy(
        src_ref=source, dst_ref=target, send_sem=send_sem, recv_sem=recv_sem,
        device_id=device, device_id_type=MESH,
    )
    copy.start()
    return copy


def reduce(groups, total, sending, landing, gathered, send_sems, recv_sems, sent):
    def go(source, target, device):
        n = len(sent)
        sent.append(send(source, target, send_sems.at[n], recv_sems.at[n], device))
        return sent[-1]

    start, extent, place, bases = 0, total.shape[0], 0, []
    for size, here, others in groups:
        sending[place : place + extent, :] = total[pl.ds(start, extent), :].astype(BF16)
        part = extent // size
        copies = []
        for d, (index, device) in enumerate(others):
            source = sending.at[pl.ds(pl.multiple_of(place + index * part, 16), part)]
            copies.append(go(source, landing.at[pl.ds(place + d * part, part)], device))
        yield
        bases.append((start, extent))
        start = pl.multiple_of(start + here * part, 16)
        for copy in copies:
            copy.wait_recv()
        add = total[pl.ds(start, part), :]
        for d in range(len(others)):
            add = add + landing[place + d * part : place + (d + 1) * part, :].astype(F32)
        total[pl.ds(start, part), :] = add
        place += extent
        extent = part
    gathered[pl.ds(start, extent), :] = total[pl.ds(start, extent), :].astype(BF16)
    for n in range(len(groups) - 1, -1, -1):
        mine = gathered.at[pl.ds(start, extent)]
        copies = [go(mine, mine, device) for _, device in groups[n][2]]
        yield
        for copy in copies:
            copy.wait_recv()
        start, extent = bases[n]


def step_kernel(
    space_count, peers, cap,
    nbrs_ref, reads_ref, counts_ref, feat_ref, pos_ref, probe_ref, target_ref, atom_filter_ref, probe_filter_ref,
    mix_ref, readout_ref,
    density_ref, probe_sum_ref, atom_sum_ref,
    around, where_ref, keeps, places, region, notes_ref, notes, sources, targets, square, atom_rad, sums, message, updated, table, index,
    sent, replies, read_where, wide, probe_rad, summed, grads, backs, sent_back, returned,
    probe_total, probe_sending, probe_landing, atom_total, atom_sending, atom_landing,
    near_sems, tile_sems, reply_sems, return_sems, probe_sems, atom_sems, table_sem,
):
    blocks, channels, width = feat_ref.shape
    _, tiles, probes = probe_ref.shape
    filters = atom_filter_ref.shape[1] // channels
    nbrs = nbrs_ref.shape[0]
    reads = reads_ref.shape[1]
    own = tiles * reads
    slots = peers * cap
    s, t = lax.axis_index("space"), lax.axis_index("tile")
    low, high = (s + space_count - 1) % space_count, (s + 1) % space_count
    core = s % 2
    sibling = s - core + (1 - core)
    chips = space_count // 2
    row = s // 2
    hops = sorted(range(1, peers), key=lambda d: -min(d, peers - d))
    tile_peers = [(t + d) % peers for d in hops]
    row_peers = [(row + d) % chips for d in range(1, chips)]
    pair_group = (2, core, [(1 - core, {"space": sibling})])
    row_group = (chips, row, [(r, {"space": r * 2 + core}) for r in row_peers])
    tile_group = (peers, t, [(p, {"tile": p}) for p in tile_peers])
    chip_list = []
    for a in range(chips):
        for b in range(peers):
            if a or b:
                r, p = (row + a) % chips, (t + b) % peers
                chip_list.append((r * peers + p, {"space": r * 2 + core, "tile": p}))
    chip_group = (chips * peers, row * peers + t, chip_list)

    barrier = pltpu.get_barrier_semaphore()
    greeted = [{"space": low}, {"space": high}, {"space": sibling}] + [d for _, d in chip_list]
    for device in greeted:
        pl.semaphore_signal(barrier, inc=1, device_id=device, device_id_type=MESH)
    lane = lax.broadcasted_iota(jnp.int32, (1, width), 1)
    keep = [jnp.where(lane < counts_ref[b], 1.0, 0.0) for b in range(blocks)]
    for b in range(blocks):
        keeps[b] = jnp.broadcast_to(keep[b], (8, width))
        around[blocks + b] = (feat_ref[b].astype(F32) * keep[b]).astype(BF16)
    pos = [pos_ref[c].astype(F32) for c in range(3)]
    for b in range(0, blocks, 4):
        rows = [part[n : n + 1] if c < 3 else keep[n] for n in range(b, b + 4) for c, part in enumerate(pos + [keep])]
        where_ref[4 * b : 4 * b + 16, :] = jnp.concatenate(rows, axis=0).astype(BF16)
    sub = lax.broadcasted_iota(jnp.int32, notes_ref.shape, 0)
    lane = lax.broadcasted_iota(jnp.int32, notes_ref.shape, 1)
    note = jnp.zeros(notes_ref.shape, jnp.int32)
    flat = [lax.rem(reads_ref[n // reads, n % reads], peers * blocks) for n in range(own)]
    for n in range(own):
        value = jnp.where(sub == 0, flat[n], jnp.where(sub == 1, lax.div(flat[n], blocks), 0))
        value = jnp.where(sub == 2, t, jnp.where(sub == 3, n // reads, jnp.where(sub == 4, n % reads, value)))
        note = jnp.where(lane == t * own + n, value, note)
    notes_ref[...] = note
    region[pl.ds(pl.multiple_of(t * 4 * blocks, 16), 4 * blocks), :] = where_ref[...]
    notes[t] = notes_ref[...]
    pl.semaphore_wait(barrier, len(greeted))

    place_copies = [
        send(where_ref, places.at[1], near_sems.at[0, 0], near_sems.at[1, 0], {"space": low}),
        send(where_ref, places.at[0], near_sems.at[0, 1], near_sems.at[1, 1], {"space": high}),
    ]
    feat_copies = [
        send(
            around.at[pl.ds(blocks, blocks)], around.at[pl.ds(2 * blocks, blocks)],
            near_sems.at[0, 2], near_sems.at[1, 2], {"space": low},
        ),
        send(
            around.at[pl.ds(blocks, blocks)], around.at[pl.ds(0, blocks)],
            near_sems.at[0, 3], near_sems.at[1, 3], {"space": high},
        ),
    ]
    tile_copies = []
    for d, p in enumerate(tile_peers):
        mine = pl.ds(pl.multiple_of(t * 4 * blocks, 16), 4 * blocks)
        tile_copies.append(
            send(notes_ref, notes.at[t], tile_sems.at[0, 2 * d], tile_sems.at[1, 2 * d], {"tile": p})
        )
        tile_copies.append(
            send(where_ref, region.at[mine], tile_sems.at[0, 2 * d + 1], tile_sems.at[1, 2 * d + 1], {"tile": p})
        )

    for b in range(blocks):
        where = where_ref[4 * b : 4 * b + 4, :].astype(F32)
        sources[blocks + b] = source_rows(where)
        targets[b] = target_rows(where)
    for copy in place_copies:
        copy.wait_recv()
    for side in range(2):
        for b in range(blocks):
            where = places[side, 4 * b : 4 * b + 4, :].astype(F32)
            sources[2 * blocks * side + b] = source_rows(where)

    def near(b, k):
        block = nbrs_ref[k, b]
        side = lax.rem(lax.div(block, peers * blocks) + (space_count + 1) - s, space_count)
        return within(side * blocks + lax.rem(block, blocks), 3 * blocks - 1)

    factor = (nbrs * width) ** (-0.5)
    chunk = 32

    def atom_radial(b, carry):
        rows = [sources[near(b, k)] for k in range(nbrs)]
        square[...] = dot_tn(jnp.concatenate(rows, axis=1), targets[b])

        def fill(step, carry):
            at = pl.ds(pl.multiple_of(step * chunk, chunk), chunk)
            for r, value in enumerate(radial(square[at, :], factor, filters)):
                atom_rad[b, at, r * width : (r + 1) * width] = value.astype(BF16)
            return carry

        return lax.fori_loop(0, nbrs * width // chunk, fill, carry, unroll=8)

    lax.fori_loop(0, blocks, atom_radial, 0)

    for copy in tile_copies:
        copy.wait_recv()
    rows = notes[0]
    for p in range(1, peers):
        rows = rows + notes[p]
    table[...] = slot_tables(rows.astype(F32), t.astype(F32), peers, cap, blocks, reads)
    to_scalars = pltpu.make_async_copy(table, index, table_sem)
    to_scalars.start()
    to_scalars.wait()
    shape = (region.shape[0], own * 8)
    lane = lax.broadcasted_iota(jnp.int32, (1, own * 8), 1)
    part = jnp.bitwise_and(lane, 7)
    want = jnp.full((1, own * 8), -8, jnp.int32)
    for n in range(own):
        want = jnp.where(jnp.logical_and(lane >= 8 * n, lane < 8 * n + 4), 4 * flat[n] + part, want)
    pick = jnp.where(lax.broadcasted_iota(jnp.int32, shape, 0) == want, 1.0, 0.0).astype(BF16)
    read_where[...] = dot_tn(pick, region[...])

    for copy in feat_copies:
        copy.wait_recv()

    def atom_layer(b, carry):
        feats = jnp.concatenate([around[near(b, k)] for k in range(nbrs)], axis=1)
        at = pl.ds(pl.multiple_of(b * width, width), width)
        for r in range(0, filters, 2):
            part = dot(feats, atom_rad[b, :, r * width : (r + 2) * width])
            sums[r * channels : (r + 1) * channels, at] = part[:, :width].astype(BF16)
            sums[(r + 1) * channels : (r + 2) * channels, at] = part[:, width:].astype(BF16)
        out = dot(atom_filter_ref[...], sums[:, at])
        message[b] = out
        own = around[blocks + b].astype(F32)
        keep = keeps[b][:1, :]
        updated[b] = (own + out * jax.nn.sigmoid(out) * keep).astype(BF16)
        return carry

    lax.fori_loop(0, blocks, atom_layer, 0, unroll=2)

    for slot in range(slots):
        sent[slot] = updated[within(index[0, slot], blocks - 1)]
    mine = pl.ds(t * cap, cap)
    reply_copies = []
    for d, p in enumerate(tile_peers):
        reply_copies.append(
            send(sent.at[pl.ds(p * cap, cap)], replies.at[mine], reply_sems.at[0, d], reply_sems.at[1, d], {"tile": p})
        )
    replies[mine] = sent[mine]
    probe_factor = (reads * width) ** (-0.5)
    span = min(256, probes)
    for tile in range(tiles):
        rows = [
            source_rows(read_where[(tile * reads + k) * 8 : (tile * reads + k + 1) * 8, :]) for k in range(reads)
        ]
        wide[...] = dot_tn(jnp.concatenate(rows, axis=1), target_rows(jnp.concatenate([probe_ref[c, tile : tile + 1, :] for c in range(3)], axis=0)))

        def fill(step, carry, tile=tile):
            at = pl.ds(pl.multiple_of(step * 16, 16), 16)
            for p in range(0, probes, span):
                for r, value in enumerate(radial(wide[at, p : p + span], probe_factor, filters)):
                    probe_rad[tile, at, r * probes + p : r * probes + p + span] = value.astype(BF16)
            return carry

        lax.fori_loop(0, reads * width // 16, fill, 0, unroll=4)
    for copy in reply_copies:
        copy.wait_recv()

    readout = jnp.broadcast_to(readout_ref[...], (8, channels)).T[:, :1]
    backs[0] = jnp.zeros_like(backs[0])
    grad_filter = grad_mix = grad_readout = None
    for tile in range(tiles):
        feats = jnp.concatenate(
            [replies[within(index[1, (t * tiles + tile) * reads + k], slots - 1)] for k in range(reads)], axis=1
        )

        def forward(r, carry, tile=tile, feats=feats):
            at = pl.ds(pl.multiple_of(r * probes, probes), probes)
            part = dot(feats, probe_rad[tile, :, at])
            summed[tile, pl.ds(pl.multiple_of(r * channels, channels), channels), :] = part.astype(BF16)
            return carry

        lax.fori_loop(0, filters, forward, 0)
        hidden = dot(probe_filter_ref[...], summed[tile])
        gate = jax.nn.sigmoid(hidden)
        squashed = (hidden * gate).astype(BF16)
        mixed = dot(mix_ref[...], squashed)
        mixed_gate = jax.nn.sigmoid(mixed)
        outer = mixed * mixed_gate
        density = jnp.sum(readout * outer, axis=0, keepdims=True)
        density_ref[tile : tile + 1, :] = density
        misfit = (density - target_ref[tile : tile + 1, :]) / probes
        part = jnp.sum(outer * misfit, axis=1, keepdims=True)
        part = jnp.broadcast_to(part, (channels, channels)).T[:16, :]
        grad_readout = part if grad_readout is None else grad_readout + part
        grad_mixed = (readout * misfit * (mixed_gate * (1.0 + mixed * (1.0 - mixed_gate)))).astype(BF16)
        part = dot_nt(grad_mixed, squashed)
        grad_mix = part if grad_mix is None else grad_mix + part
        grad_squashed = dot_tn(mix_ref[...], grad_mixed)
        grad_hidden = (grad_squashed * (gate * (1.0 + hidden * (1.0 - gate)))).astype(BF16)
        part = dot_nt(grad_hidden, summed[tile])
        for r in range(filters):
            at = slice(r * channels, (r + 1) * channels)
            piece = part[:, at]
            probe_total[at, :] = piece if tile == 0 else probe_total[at, :] + piece
        for r in range(filters):
            piece = dot_tn(probe_filter_ref[:, r * channels : (r + 1) * channels], grad_hidden)
            grads[:, r * probes : (r + 1) * probes] = piece.astype(BF16)
        for k in range(0, reads, 2):
            back = dot_nt(grads[...], probe_rad[tile, k * width : (k + 2) * width, :])
            for n in range(2):
                backs[1 + tile * reads + k + n] = back[:, n * width : (n + 1) * width]
    base = filters * channels
    probe_total[base : base + channels, :] = grad_mix
    probe_total[base + channels : base + channels + 16, :] = grad_readout
    spare = probe_total.shape[0] - base - channels - 16
    if spare:
        probe_total[base + channels + 16 :, :] = jnp.zeros((spare, channels), F32)

    probe_copies, atom_copies = [], []
    probe_steps = reduce(
        [pair_group, row_group, tile_group], probe_total, probe_sending, probe_landing, probe_sum_ref,
        probe_sems.at[0], probe_sems.at[1], probe_copies,
    )
    atom_steps = reduce(
        [pair_group, chip_group], atom_total, atom_sending, atom_landing, atom_sum_ref,
        atom_sems.at[0], atom_sems.at[1], atom_copies,
    )
    next(probe_steps)

    for slot in range(slots):
        total = backs[within(index[3, slot], reads)]
        for tile in range(1, tiles):
            place = within(index[3, tile * slots + slot], reads)
            total = total + backs[jnp.where(place > 0, place + tile * reads, 0)]
        sent_back[slot] = total.astype(BF16)
    step = cap + 1
    landing = pl.ds(t * step + 1, cap)
    next(probe_steps)
    return_copies = []
    for d, p in enumerate(tile_peers):
        return_copies.append(
            send(
                sent_back.at[pl.ds(p * cap, cap)], returned.at[landing],
                return_sems.at[0, d], return_sems.at[1, d], {"tile": p},
            )
        )
    for p in range(peers):
        returned[p * step] = jnp.zeros((channels, width), BF16)
    returned[landing] = sent_back[mine]
    next(probe_steps)
    for copy in return_copies:
        copy.wait_recv()

    def atom_grad(b, carry):
        total = None
        for p in range(peers):
            part = returned[p * step + within(index[2, p * blocks + b], cap)].astype(F32)
            total = part if total is None else total + part
        grad = total * keeps[b][:1, :] * silu_slope(message[b])
        grads[:, pl.ds(pl.multiple_of(b * width, width), width)] = grad.astype(BF16)
        return carry

    lax.fori_loop(0, blocks, atom_grad, 0, unroll=2)
    for r in range(0, filters, 2):
        part = dot_nt(grads[:, : blocks * width], sums[r * channels : (r + 2) * channels, :])
        for n in range(2):
            at = slice((r + n) * channels, (r + n + 1) * channels)
            atom_total[at, :] = part[:, n * channels : (n + 1) * channels]
    spare = atom_total.shape[0] - base
    if spare:
        atom_total[base:, :] = jnp.zeros((spare, channels), F32)
    turn = [atom_steps, probe_steps]
    while turn:
        turn = [steps for steps in turn if next(steps, 0) is None]
    every = place_copies + feat_copies + tile_copies + reply_copies + return_copies + probe_copies + atom_copies
    for copy in every:
        copy.wait_send()


def unpack_kernel(density_ref, probe_ref, atom_ref, out_ref, grad_atom_ref, grad_probe_ref, grad_mix_ref, readout_ref):
    channels = grad_mix_ref.shape[0]
    filters = grad_atom_ref.shape[1] // channels
    out_ref[...] = density_ref[...]
    for r in range(filters):
        at = slice(r * channels, (r + 1) * channels)
        grad_atom_ref[:, at] = atom_ref[at, :].astype(F32)
        grad_probe_ref[:, at] = probe_ref[at, :].astype(F32)
    base = filters * channels
    grad_mix_ref[...] = probe_ref[base : base + channels, :].astype(F32)
    readout_ref[...] = probe_ref[base + channels : base + channels + 16, :].astype(F32)[:1]


def body(
    atom_feat, atom_pos, atom_counts, atom_nbrs, probe_pos, probe_target, tile_blocks,
    atom_filter, probe_filter, mix_weight, readout,
):
    blocks, channels, width = atom_feat.shape
    tiles, reads = tile_blocks.shape
    probes = probe_pos.shape[2]
    filters = atom_filter.shape[1] // channels
    nbrs = atom_nbrs.shape[1]
    peers = lax.axis_size("tile")
    space_count = lax.axis_size("space")
    devices = peers * space_count
    cap = max(2, 2 * reads * tiles // peers)
    slots = peers * cap
    own = tiles * reads
    lanes = max(peers * own, peers * blocks, tiles * slots)
    unit = 16 * devices
    atom_rows = -(-filters * channels // unit) * unit
    probe_rows = -(-(filters * channels + channels + 16) // unit) * unit
    vmem = pl.BlockSpec(memory_space=pltpu.VMEM)
    smem = pl.BlockSpec(memory_space=pltpu.SMEM)
    dma = pltpu.SemaphoreType.DMA
    chips = space_count // 2
    probe_space = probe_rows + probe_rows // 2 + probe_rows // (2 * chips)
    density, probe_sum, atom_sum = pl.pallas_call(
        functools.partial(step_kernel, space_count, peers, cap),
        in_specs=[smem] * 3 + [vmem] * 8,
        out_specs=[vmem] * 3,
        out_shape=[
            jax.ShapeDtypeStruct((tiles, probes), F32),
            jax.ShapeDtypeStruct((probe_rows, channels), BF16),
            jax.ShapeDtypeStruct((atom_rows, channels), BF16),
        ],
        scratch_shapes=[
            pltpu.VMEM((3 * blocks, channels, width), BF16),
            pltpu.VMEM((4 * blocks, width), BF16),
            pltpu.VMEM((blocks, 8, width), F32),
            pltpu.VMEM((2, 4 * blocks, width), BF16),
            pltpu.VMEM((peers * 4 * blocks, width), BF16),
            pltpu.VMEM((8, lanes), jnp.int32),
            pltpu.VMEM((peers, 8, lanes), jnp.int32),
            pltpu.VMEM((3 * blocks, 16, width), BF16),
            pltpu.VMEM((blocks, 16, width), BF16),
            pltpu.VMEM((nbrs * width, width), F32),
            pltpu.VMEM((blocks, nbrs * width, filters * width), BF16),
            pltpu.VMEM((filters * channels, blocks * width), BF16),
            pltpu.VMEM((blocks, channels, width), F32),
            pltpu.VMEM((blocks, channels, width), BF16),
            pltpu.VMEM((8, lanes), jnp.int32),
            pltpu.SMEM((8, lanes), jnp.int32),
            pltpu.VMEM((slots, channels, width), BF16),
            pltpu.VMEM((slots, channels, width), BF16),
            pltpu.VMEM((own * 8, width), F32),
            pltpu.VMEM((reads * width, probes), F32),
            pltpu.VMEM((tiles, reads * width, filters * probes), BF16),
            pltpu.VMEM((tiles, filters * channels, probes), BF16),
            pltpu.VMEM((channels, max(filters * probes, blocks * width)), BF16),
            pltpu.VMEM((1 + own, channels, width), F32),
            pltpu.VMEM((slots, channels, width), BF16),
            pltpu.VMEM((peers * (cap + 1), channels, width), BF16),
            pltpu.VMEM((probe_rows, channels), F32),
            pltpu.VMEM((probe_space, channels), BF16),
            pltpu.VMEM((probe_space, channels), BF16),
            pltpu.VMEM((atom_rows, channels), F32),
            pltpu.VMEM((atom_rows + atom_rows // 2, channels), BF16),
            pltpu.VMEM((atom_rows + atom_rows // 2, channels), BF16),
            dma((2, 4)),
            dma((2, 2 * (peers - 1))),
            dma((2, peers - 1)),
            dma((2, peers - 1)),
            dma((2, 2 * (1 + chips - 1 + peers - 1))),
            dma((2, 2 * (1 + chips * peers - 1))),
            dma,
        ],
        compiler_params=pltpu.CompilerParams(
            vmem_limit_bytes=VMEM_LIMIT, collective_id=0, has_side_effects=True
        ),
        name="network_step",
    )(
        atom_nbrs.T, tile_blocks, atom_counts, atom_feat, atom_pos.transpose(1, 0, 2), probe_pos.transpose(1, 0, 2),
        probe_target, atom_filter, probe_filter, mix_weight,
        readout.reshape(1, channels),
    )
    density, grad_atom, grad_probe, grad_mix, grad_readout = pl.pallas_call(
        unpack_kernel,
        in_specs=[vmem] * 3,
        out_specs=[vmem] * 5,
        out_shape=[
            jax.ShapeDtypeStruct((tiles, probes), F32),
            jax.ShapeDtypeStruct((channels, filters * channels), F32),
            jax.ShapeDtypeStruct((channels, filters * channels), F32),
            jax.ShapeDtypeStruct((channels, channels), F32),
            jax.ShapeDtypeStruct((1, channels), F32),
        ],
        name="unpack",
    )(density, probe_sum, atom_sum)
    return density, grad_atom, grad_probe, grad_mix, grad_readout.reshape(channels)


def solution(mesh):
    return jax.shard_map(
        body,
        mesh=mesh,
        in_specs=(
            P(("space", "tile"), None, None),
            P(("space", "tile"), None, None),
            P(("space", "tile")),
            P(("space", "tile"), None),
            P(("space", "tile"), None, None),
            P(("space", "tile"), None),
            P(("space", "tile"), None),
            P(),
            P(),
            P(),
            P(),
        ),
        out_specs=(P(("space", "tile"), None), P(), P(), P(), P()),
        check_vma=False,
    )
```

```python
import functools
import math

import jax
import jax.numpy as jnp
from jax import lax
from jax.experimental import pallas as pl
from jax.experimental.pallas import tpu as pltpu
from jax.sharding import PartitionSpec as P

CUTOFF = 6.0
SPACING = 0.75
SPREAD = 0.75
LOG2E = 1.4426950408889634
MESH = pl.DeviceIdType.MESH
VMEM_LIMIT = 60 * 1024 * 1024
F32 = jnp.float32
BF16 = jnp.bfloat16
KAPPA = 2.0 * SPACING / SPREAD / SPREAD * LOG2E
BUMP = (0.9999997912905728, -0.23369419608566247, 0.01993802762546961, -0.0008456218103791793)


def silu_slope(values):
    s = jax.nn.sigmoid(values)
    return s * (1.0 + values * (1.0 - s))


def dot(a, b):
    return jnp.dot(a, b, preferred_element_type=F32)


def dot_nt(a, b):
    return lax.dot_general(a, b, (((1,), (1,)), ((), ())), preferred_element_type=F32)


def dot_tn(a, b):
    return lax.dot_general(a, b, (((0,), (0,)), ((), ())), preferred_element_type=F32)


def radial(square, factor, filters):
    middle = filters // 2
    step = SPACING / SPREAD
    edge = (CUTOFF * KAPPA) ** 2
    base = [
        math.sqrt(factor) * math.exp(-0.5 * (middle * step) ** 2) * c / edge ** (k + 1)
        for k, c in enumerate(BUMP)
    ]
    reach = square * lax.rsqrt(square)
    up = jnp.exp2(reach - (2 * middle + 1) * step * step * LOG2E)
    down = jnp.exp2((2 * middle - 1) * step * step * LOG2E - reach)
    bell = jnp.exp2(square * (-LOG2E / (SPREAD * KAPPA) ** 2) + reach * float(middle))
    wave = ((base[3] * square + base[2]) * square + base[1]) * square + base[0]
    wave = wave * jnp.maximum(edge - square, 0.0)
    values = [None] * filters
    values[middle] = bell * (wave * wave)
    for r in range(middle + 1, filters):
        k = r - middle - 1
        values[r] = values[r - 1] * (up if k == 0 else up * math.exp(-2.0 * k * step * step))
    for r in range(middle - 1, -1, -1):
        k = middle - 1 - r
        values[r] = values[r + 1] * (down if k == 0 else down * math.exp(-2.0 * k * step * step))
    return values


def thirds(values):
    out = []
    for _ in range(3):
        part = values.astype(BF16).astype(F32)
        out.append(part)
        values = values - part
    return out


def source_rows(where):
    x = [where[c : c + 1] for c in range(3)]
    norm = thirds(KAPPA**2 * (x[0] * x[0] + x[1] * x[1] + x[2] * x[2]))
    one = jnp.ones_like(x[0])
    return jnp.concatenate(x * 3 + norm + [one] * 3 + [one * 0.0], axis=0).astype(BF16)


def target_rows(where):
    y = [where[c : c + 1] for c in range(3)]
    norm = thirds(KAPPA**2 * (y[0] * y[0] + y[1] * y[1] + y[2] * y[2] + 0.01))
    y = [thirds(-2.0 * KAPPA**2 * part) for part in y]
    one = jnp.ones_like(norm[0])
    rows = [y[c][k] for k in range(3) for c in range(3)] + [one] * 3 + norm + [one * 0.0]
    return jnp.concatenate(rows, axis=0).astype(BF16)


def slot_tables(rows, me, peers, cap, blocks, reads):
    lanes = rows.shape[1]
    cols = rows.T
    row = lambda n: rows[n : n + 1, :]
    col = lambda n: cols[:, n : n + 1]
    block, owner, asker, tile, place = range(5)
    down = lax.broadcasted_iota(jnp.int32, (lanes, lanes), 0)
    along = lax.broadcasted_iota(jnp.int32, (lanes, lanes), 1)
    lane = along.astype(F32)
    yes = lambda cond: jnp.where(cond, 1.0, 0.0)
    same = yes(col(asker) == row(asker))
    equal = same * yes(col(block) == row(block))
    first_row = yes(jnp.sum(equal * yes(down < along), axis=0, keepdims=True) < 0.5)
    first_col = yes(jnp.sum(equal * yes(along < down), axis=1, keepdims=True) < 0.5)
    group = same * yes(col(owner) == row(owner))
    rank_col = jnp.sum(group * yes(row(block) < col(block)) * first_row, axis=1, keepdims=True)
    rank_row = jnp.sum(group * yes(col(block) < row(block)) * first_col, axis=0, keepdims=True)
    mine = yes(col(owner) == me) * first_col
    spot = col(block) - me * float(blocks)
    led_row = yes(jnp.sum(yes(spot == lane) * mine * yes(rank_col < 0.5), axis=0, keepdims=True) > 0.5)
    mine_row = yes(row(owner) == me) * first_row * yes(rank_row < 0.5)
    depth = down.astype(F32)
    led_col = yes(
        jnp.sum(yes(row(block) - me * float(blocks) == depth) * mine_row, axis=1, keepdims=True) > 0.5
    )
    leaders = jnp.sum(led_col, axis=0, keepdims=True)
    ahead_row = jnp.sum(led_col * yes(down < along), axis=0, keepdims=True)
    ahead_col = jnp.sum(led_row * yes(along < down), axis=1, keepdims=True)
    turn_row = led_row * ahead_row + (1.0 - led_row) * (leaders + lane[:1] - ahead_row)
    turn_col = led_col * ahead_col + (1.0 - led_col) * (leaders + depth[:, :1] - ahead_col)
    spot = jnp.sum(yes(spot == lane) * turn_row, axis=1, keepdims=True)
    put = lambda cond, value: jnp.sum(yes(cond) * value, axis=0, keepdims=True)
    asked = put(col(asker) * cap + rank_col == lane, mine * spot)
    slot = row(owner) * cap + rank_row
    arrival = put(col(asker) * blocks + spot == lane, mine * (rank_col + 1.0))
    slot_col = col(owner) * cap + rank_col
    own = yes(col(asker) == me)
    fill = put(col(tile) * (peers * cap) + slot_col == lane, own * (col(place) + 1.0))
    work = put(turn_col == lane, yes(depth[:, :1] < blocks) * depth[:, :1])
    limit = lambda value, most: jnp.clip(value, 0.0, float(most))
    rows = [
        limit(asked, blocks - 1), limit(slot, peers * cap - 1), limit(arrival, cap), limit(fill, reads),
        limit(work, blocks - 1), jnp.zeros((3, lanes), F32),
    ]
    return jnp.concatenate(rows, axis=0).astype(jnp.int32)


def within(value, most):
    return jnp.minimum(jnp.maximum(value, 0), most)


def send(source, target, send_sem, recv_sem, device):
    copy = pltpu.make_async_remote_copy(
        src_ref=source, dst_ref=target, send_sem=send_sem, recv_sem=recv_sem,
        device_id=device, device_id_type=MESH,
    )
    copy.start()
    return copy


def reduce(groups, total, sending, landing, gathered, send_sems, recv_sems, sent):
    def go(source, target, device):
        n = len(sent)
        sent.append(send(source, target, send_sems.at[n], recv_sems.at[n], device))
        return sent[-1]

    start, extent, place, bases = 0, total.shape[0], 0, []
    for size, here, others in groups:
        sending[place : place + extent, :] = total[pl.ds(start, extent), :].astype(BF16)
        part = extent // size
        copies = []
        for d, (index, device) in enumerate(others):
            source = sending.at[pl.ds(pl.multiple_of(place + index * part, 16), part)]
            copies.append(go(source, landing.at[pl.ds(place + d * part, part)], device))
        yield
        bases.append((start, extent))
        start = pl.multiple_of(start + here * part, 16)
        for copy in copies:
            copy.wait_recv()
        add = total[pl.ds(start, part), :]
        for d in range(len(others)):
            add = add + landing[place + d * part : place + (d + 1) * part, :].astype(F32)
        total[pl.ds(start, part), :] = add
        place += extent
        extent = part
    gathered[pl.ds(start, extent), :] = total[pl.ds(start, extent), :].astype(BF16)
    for n in range(len(groups) - 1, -1, -1):
        mine = gathered.at[pl.ds(start, extent)]
        copies = [go(mine, mine, device) for _, device in groups[n][2]]
        yield
        for copy in copies:
            copy.wait_recv()
        start, extent = bases[n]


def step_kernel(
    space_count, peers, cap,
    nbrs_ref, reads_ref, counts_ref, feat_ref, pos_ref, probe_ref, target_ref, atom_filter_ref, probe_filter_ref,
    mix_ref, readout_ref,
    density_ref, probe_sum_ref, atom_sum_ref,
    near_feats, far_feats, where_ref, keeps, places, region, notes_ref, notes, sources, targets, square, other_square, stage, other_stage, atom_rad, partial, sums, message, updated, table, index,
    sent, replies, read_where, wide, probe_rad, summed, grads, backs, sent_back, returned,
    probe_total, probe_sending, probe_landing, atom_total, atom_sending, atom_landing,
    near_sems, tile_sems, reply_sems, return_sems, probe_sems, atom_sems, table_sem,
):
    blocks, channels, width = feat_ref.shape
    _, tiles, probes = probe_ref.shape
    filters = atom_filter_ref.shape[1] // channels
    nbrs = nbrs_ref.shape[0]
    reads = reads_ref.shape[1]
    own = tiles * reads
    slots = peers * cap
    s, t = lax.axis_index("space"), lax.axis_index("tile")
    low, high = (s + space_count - 1) % space_count, (s + 1) % space_count
    core = s % 2
    sibling = s - core + (1 - core)
    cross = (s + 2 * core - 1 + space_count) % space_count
    chips = space_count // 2
    row = s // 2
    hops = sorted(range(1, peers), key=lambda d: -min(d, peers - d))
    tile_peers = [(t + d) % peers for d in hops]
    row_peers = [(row + d) % chips for d in range(1, chips)]
    pair_group = (2, core, [(1 - core, {"space": sibling})])
    row_group = (chips, row, [(r, {"space": r * 2 + core}) for r in row_peers])
    tile_group = (peers, t, [(p, {"tile": p}) for p in tile_peers])
    chip_list = []
    for a in range(chips):
        for b in range(peers):
            if a or b:
                r, p = (row + a) % chips, (t + b) % peers
                chip_list.append((r * peers + p, {"space": r * 2 + core, "tile": p}))
    chip_group = (chips * peers, row * peers + t, chip_list)

    barrier = pltpu.get_barrier_semaphore()
    greeted = [{"space": sibling}, {"space": cross}] + [d for _, d in chip_list]
    for device in greeted:
        pl.semaphore_signal(barrier, inc=1, device_id=device, device_id_type=MESH)
    lane = lax.broadcasted_iota(jnp.int32, (1, width), 1)
    keep = [jnp.where(lane < counts_ref[b], 1.0, 0.0) for b in range(blocks)]
    for b in range(blocks):
        keeps[b] = jnp.broadcast_to(keep[b], (8, width))
        near_feats[b] = (feat_ref[b].astype(F32) * keep[b]).astype(BF16)
    pos = [pos_ref[c].astype(F32) for c in range(3)]
    for b in range(0, blocks, 4):
        rows = [part[n : n + 1] if c < 3 else keep[n] for n in range(b, b + 4) for c, part in enumerate(pos + [keep])]
        where_ref[4 * b : 4 * b + 16, :] = jnp.concatenate(rows, axis=0).astype(BF16)
    sub = lax.broadcasted_iota(jnp.int32, notes_ref.shape, 0)
    lane = lax.broadcasted_iota(jnp.int32, notes_ref.shape, 1)
    note = jnp.zeros(notes_ref.shape, jnp.int32)
    flat = [lax.rem(reads_ref[n // reads, n % reads], peers * blocks) for n in range(own)]
    for n in range(own):
        value = jnp.where(sub == 0, flat[n], jnp.where(sub == 1, lax.div(flat[n], blocks), 0))
        value = jnp.where(sub == 2, t, jnp.where(sub == 3, n // reads, jnp.where(sub == 4, n % reads, value)))
        note = jnp.where(lane == t * own + n, value, note)
    notes_ref[...] = note
    region[pl.ds(pl.multiple_of(t * 4 * blocks, 16), 4 * blocks), :] = where_ref[...]
    notes[t] = notes_ref[...]
    pl.semaphore_wait(barrier, len(greeted))

    place_copies = [
        send(where_ref, places.at[1], near_sems.at[0, 0], near_sems.at[1, 0], {"space": low}),
        send(where_ref, places.at[0], near_sems.at[0, 1], near_sems.at[1, 1], {"space": high}),
    ]
    own_feats = near_feats.at[pl.ds(0, blocks)]
    sibling_copy = send(
        own_feats, near_feats.at[pl.ds(blocks, blocks)], near_sems.at[0, 2], near_sems.at[1, 2], {"space": sibling}
    )
    cross_copy = send(own_feats, far_feats, near_sems.at[0, 3], near_sems.at[1, 3], {"space": cross})
    tile_copies = []
    for d, p in enumerate(tile_peers):
        mine = pl.ds(pl.multiple_of(t * 4 * blocks, 16), 4 * blocks)
        tile_copies.append(
            send(notes_ref, notes.at[t], tile_sems.at[0, 2 * d], tile_sems.at[1, 2 * d], {"tile": p})
        )
        tile_copies.append(
            send(where_ref, region.at[mine], tile_sems.at[0, 2 * d + 1], tile_sems.at[1, 2 * d + 1], {"tile": p})
        )

    for b in range(blocks):
        where = where_ref[4 * b : 4 * b + 4, :].astype(F32)
        sources[blocks + b] = source_rows(where)
        targets[b] = target_rows(where)
    for copy in place_copies:
        copy.wait_recv()
    for side in range(2):
        for b in range(blocks):
            where = places[side, 4 * b : 4 * b + 4, :].astype(F32)
            sources[2 * blocks * side + b] = source_rows(where)

    order = [1 - core, 2, core] + list(range(3, nbrs))
    half = 2 * width

    def spot(b, k):
        return within(lax.rem(nbrs_ref[k, b], blocks), blocks - 1)

    def side(b, k):
        block = nbrs_ref[k, b]
        return lax.rem(lax.div(block, peers * blocks) + (space_count + 1) - s, space_count)

    factor = (nbrs * width) ** (-0.5)
    chunk = 32

    def atom_radial(b, square, stage):
        rows = [sources[within(side(b, k) * blocks + spot(b, k), 3 * blocks - 1)] for k in order]
        square[...] = dot_tn(jnp.concatenate(rows, axis=1), targets[b])
        for low in range(0, nbrs * width, chunk):
            for r, value in enumerate(radial(square[low : low + chunk, :], factor, filters)):
                at = slice(r * width, (r + 1) * width)
                if low < half:
                    stage[low : low + chunk, at] = value.astype(BF16)
                else:
                    atom_rad[b, low - half : low - half + chunk, at] = value.astype(BF16)

    def near_part(b, stage):
        feats = jnp.concatenate(
            [near_feats[blocks + spot(b, order[0])], near_feats[spot(b, order[1])]], axis=1
        )
        for r in range(0, filters, 2):
            at = slice(r * width, (r + 2) * width)
            partial[b, :, at] = dot(feats, stage[:, at])

    def two_blocks(n, carry):
        b = 2 * n
        near_part(b, stage)
        atom_radial(b + 1, other_square, other_stage)
        near_part(b + 1, other_stage)
        atom_radial(b + 2, square, stage)
        return carry

    sibling_copy.wait_recv()
    atom_radial(0, square, stage)
    lax.fori_loop(0, blocks // 2 - 1, two_blocks, 0)
    near_part(blocks - 2, stage)
    atom_radial(blocks - 1, other_square, other_stage)
    near_part(blocks - 1, other_stage)

    for copy in tile_copies:
        copy.wait_recv()
    rows = notes[0]
    for p in range(1, peers):
        rows = rows + notes[p]
    table[...] = slot_tables(rows.astype(F32), t.astype(F32), peers, cap, blocks, reads)
    to_scalars = pltpu.make_async_copy(table, index, table_sem)
    to_scalars.start()
    to_scalars.wait()
    shape = (region.shape[0], own * 8)
    lane = lax.broadcasted_iota(jnp.int32, (1, own * 8), 1)
    part = jnp.bitwise_and(lane, 7)
    want = jnp.full((1, own * 8), -8, jnp.int32)
    for n in range(own):
        want = jnp.where(jnp.logical_and(lane >= 8 * n, lane < 8 * n + 4), 4 * flat[n] + part, want)
    pick = jnp.where(lax.broadcasted_iota(jnp.int32, shape, 0) == want, 1.0, 0.0).astype(BF16)
    read_where[...] = dot_tn(pick, region[...])

    cross_copy.wait_recv()

    def atom_layer(n, carry):
        b = within(index[4, n], blocks - 1)
        parts = [far_feats[spot(b, order[2])]]
        for k in order[3:]:
            from_far = jnp.where(side(b, k) == 2 * core, 1.0, 0.0)
            row = jnp.where(side(b, k) == 1, spot(b, k), blocks + spot(b, k))
            here = near_feats[within(row, 2 * blocks - 1)].astype(F32)
            there = far_feats[spot(b, k)].astype(F32)
            parts.append((there * from_far + here * (1.0 - from_far)).astype(BF16))
        feats = jnp.concatenate(parts, axis=1)
        at = pl.ds(pl.multiple_of(n * width, width), width)
        for r in range(0, filters, 2):
            part = dot(feats, atom_rad[b, :, r * width : (r + 2) * width])
            part = part + partial[b, :, r * width : (r + 2) * width]
            sums[r * channels : (r + 1) * channels, at] = part[:, :width].astype(BF16)
            sums[(r + 1) * channels : (r + 2) * channels, at] = part[:, width:].astype(BF16)
        out = dot(atom_filter_ref[...], sums[:, at])
        message[n] = out
        own = near_feats[b].astype(F32)
        keep = keeps[b][:1, :]
        updated[n] = (own + out * jax.nn.sigmoid(out) * keep).astype(BF16)
        return carry

    first = min(peers, blocks)
    reply_copies = []

    def reply(low, high):
        for p in range(peers):
            for slot in range(p * cap + low, p * cap + high):
                sent[slot] = updated[within(index[0, slot], blocks - 1)]
        for p in tile_peers:
            d = len(reply_copies)
            reply_copies.append(
                send(
                    sent.at[pl.ds(p * cap + low, high - low)], replies.at[pl.ds(t * cap + low, high - low)],
                    reply_sems.at[0, d], reply_sems.at[1, d], {"tile": p},
                )
            )

    lax.fori_loop(0, first, atom_layer, 0, unroll=2)
    reply(0, 1)
    lax.fori_loop(first, blocks, atom_layer, 0, unroll=2)
    reply(1, cap)

    mine = pl.ds(t * cap, cap)
    replies[mine] = sent[mine]
    probe_factor = (reads * width) ** (-0.5)
    span = min(256, probes)
    for tile in range(tiles):
        rows = [
            source_rows(read_where[(tile * reads + k) * 8 : (tile * reads + k + 1) * 8, :]) for k in range(reads)
        ]
        wide[...] = dot_tn(jnp.concatenate(rows, axis=1), target_rows(jnp.concatenate([probe_ref[c, tile : tile + 1, :] for c in range(3)], axis=0)))

        def fill(step, carry, tile=tile):
            at = pl.ds(pl.multiple_of(step * 16, 16), 16)
            for p in range(0, probes, span):
                for r, value in enumerate(radial(wide[at, p : p + span], probe_factor, filters)):
                    probe_rad[tile, at, r * probes + p : r * probes + p + span] = value.astype(BF16)
            return carry

        lax.fori_loop(0, reads * width // 16, fill, 0, unroll=4)
    for copy in reply_copies:
        copy.wait_recv()

    readout = jnp.broadcast_to(readout_ref[...], (8, channels)).T[:, :1]
    backs[0] = jnp.zeros_like(backs[0])
    grad_filter = grad_mix = grad_readout = None
    for tile in range(tiles):
        feats = jnp.concatenate(
            [replies[within(index[1, (t * tiles + tile) * reads + k], slots - 1)] for k in range(reads)], axis=1
        )

        def forward(r, carry, tile=tile, feats=feats):
            at = pl.ds(pl.multiple_of(r * probes, probes), probes)
            part = dot(feats, probe_rad[tile, :, at])
            summed[pl.ds(pl.multiple_of(r * channels, channels), channels), :] = part.astype(BF16)
            return carry

        lax.fori_loop(0, filters, forward, 0)
        hidden = dot(probe_filter_ref[...], summed[...])
        gate = jax.nn.sigmoid(hidden)
        squashed = (hidden * gate).astype(BF16)
        mixed = dot(mix_ref[...], squashed)
        mixed_gate = jax.nn.sigmoid(mixed)
        outer = mixed * mixed_gate
        density = jnp.sum(readout * outer, axis=0, keepdims=True)
        density_ref[tile : tile + 1, :] = density
        misfit = (density - target_ref[tile : tile + 1, :]) / probes
        part = jnp.sum(outer * misfit, axis=1, keepdims=True)
        part = jnp.broadcast_to(part, (channels, channels)).T[:16, :]
        grad_readout = part if grad_readout is None else grad_readout + part
        grad_mixed = (readout * misfit * (mixed_gate * (1.0 + mixed * (1.0 - mixed_gate)))).astype(BF16)
        part = dot_nt(grad_mixed, squashed)
        grad_mix = part if grad_mix is None else grad_mix + part
        grad_squashed = dot_tn(mix_ref[...], grad_mixed)
        grad_hidden = (grad_squashed * (gate * (1.0 + hidden * (1.0 - gate)))).astype(BF16)
        part = dot_nt(grad_hidden, summed[...])
        for r in range(filters):
            at = slice(r * channels, (r + 1) * channels)
            piece = part[:, at]
            probe_total[at, :] = piece if tile == 0 else probe_total[at, :] + piece
        for r in range(filters):
            piece = dot_tn(probe_filter_ref[:, r * channels : (r + 1) * channels], grad_hidden)
            grads[:, r * probes : (r + 1) * probes] = piece.astype(BF16)
        for k in range(0, reads, 2):
            back = dot_nt(grads[...], probe_rad[tile, k * width : (k + 2) * width, :])
            for n in range(2):
                backs[1 + tile * reads + k + n] = back[:, n * width : (n + 1) * width]
    base = filters * channels
    probe_total[base : base + channels, :] = grad_mix
    probe_total[base + channels : base + channels + 16, :] = grad_readout
    spare = probe_total.shape[0] - base - channels - 16
    if spare:
        probe_total[base + channels + 16 :, :] = jnp.zeros((spare, channels), F32)

    probe_copies, atom_copies = [], []
    probe_steps = reduce(
        [pair_group, row_group, tile_group], probe_total, probe_sending, probe_landing, probe_sum_ref,
        probe_sems.at[0], probe_sems.at[1], probe_copies,
    )
    atom_steps = reduce(
        [pair_group, chip_group], atom_total, atom_sending, atom_landing, atom_sum_ref,
        atom_sems.at[0], atom_sems.at[1], atom_copies,
    )
    next(probe_steps)

    for slot in range(slots):
        total = backs[within(index[3, slot], reads)]
        for tile in range(1, tiles):
            place = within(index[3, tile * slots + slot], reads)
            total = total + backs[jnp.where(place > 0, place + tile * reads, 0)]
        sent_back[slot] = total.astype(BF16)
    step = cap + 1
    landing = pl.ds(t * step + 1, cap)
    next(probe_steps)
    return_copies = []
    for d, p in enumerate(tile_peers):
        return_copies.append(
            send(
                sent_back.at[pl.ds(p * cap, cap)], returned.at[landing],
                return_sems.at[0, d], return_sems.at[1, d], {"tile": p},
            )
        )
    for p in range(peers):
        returned[p * step] = jnp.zeros((channels, width), BF16)
    returned[landing] = sent_back[mine]
    next(probe_steps)
    for copy in return_copies:
        copy.wait_recv()

    def atom_grad(b, carry):
        total = None
        for p in range(peers):
            part = returned[p * step + within(index[2, p * blocks + b], cap)].astype(F32)
            total = part if total is None else total + part
        grad = total * keeps[within(index[4, b], blocks - 1)][:1, :] * silu_slope(message[b])
        grads[:, pl.ds(pl.multiple_of(b * width, width), width)] = grad.astype(BF16)
        return carry

    lax.fori_loop(0, blocks, atom_grad, 0, unroll=2)
    for r in range(0, filters, 2):
        part = dot_nt(grads[:, : blocks * width], sums[r * channels : (r + 2) * channels, :])
        for n in range(2):
            at = slice((r + n) * channels, (r + n + 1) * channels)
            atom_total[at, :] = part[:, n * channels : (n + 1) * channels]
    spare = atom_total.shape[0] - base
    if spare:
        atom_total[base:, :] = jnp.zeros((spare, channels), F32)
    turn = [atom_steps, probe_steps]
    while turn:
        turn = [steps for steps in turn if next(steps, 0) is None]
    every = place_copies + [sibling_copy, cross_copy] + tile_copies + reply_copies + return_copies + probe_copies + atom_copies
    for copy in every:
        copy.wait_send()


def unpack_kernel(density_ref, probe_ref, atom_ref, out_ref, grad_atom_ref, grad_probe_ref, grad_mix_ref, readout_ref):
    channels = grad_mix_ref.shape[0]
    filters = grad_atom_ref.shape[1] // channels
    out_ref[...] = density_ref[...]
    for r in range(filters):
        at = slice(r * channels, (r + 1) * channels)
        grad_atom_ref[:, at] = atom_ref[at, :].astype(F32)
        grad_probe_ref[:, at] = probe_ref[at, :].astype(F32)
    base = filters * channels
    grad_mix_ref[...] = probe_ref[base : base + channels, :].astype(F32)
    readout_ref[...] = probe_ref[base + channels : base + channels + 16, :].astype(F32)[:1]


def body(
    atom_feat, atom_pos, atom_counts, atom_nbrs, probe_pos, probe_target, tile_blocks,
    atom_filter, probe_filter, mix_weight, readout,
):
    blocks, channels, width = atom_feat.shape
    tiles, reads = tile_blocks.shape
    probes = probe_pos.shape[2]
    filters = atom_filter.shape[1] // channels
    nbrs = atom_nbrs.shape[1]
    peers = lax.axis_size("tile")
    space_count = lax.axis_size("space")
    devices = peers * space_count
    cap = max(2, 2 * reads * tiles // peers)
    slots = peers * cap
    own = tiles * reads
    lanes = max(peers * own, peers * blocks, tiles * slots)
    unit = 16 * devices
    atom_rows = -(-filters * channels // unit) * unit
    probe_rows = -(-(filters * channels + channels + 16) // unit) * unit
    vmem = pl.BlockSpec(memory_space=pltpu.VMEM)
    smem = pl.BlockSpec(memory_space=pltpu.SMEM)
    dma = pltpu.SemaphoreType.DMA
    chips = space_count // 2
    probe_space = probe_rows + probe_rows // 2 + probe_rows // (2 * chips)
    density, probe_sum, atom_sum = pl.pallas_call(
        functools.partial(step_kernel, space_count, peers, cap),
        in_specs=[smem] * 3 + [vmem] * 8,
        out_specs=[vmem] * 3,
        out_shape=[
            jax.ShapeDtypeStruct((tiles, probes), F32),
            jax.ShapeDtypeStruct((probe_rows, channels), BF16),
            jax.ShapeDtypeStruct((atom_rows, channels), BF16),
        ],
        scratch_shapes=[
            pltpu.VMEM((2 * blocks, channels, width), BF16),
            pltpu.VMEM((blocks, channels, width), BF16),
            pltpu.VMEM((4 * blocks, width), BF16),
            pltpu.VMEM((blocks, 8, width), F32),
            pltpu.VMEM((2, 4 * blocks, width), BF16),
            pltpu.VMEM((peers * 4 * blocks, width), BF16),
            pltpu.VMEM((8, lanes), jnp.int32),
            pltpu.VMEM((peers, 8, lanes), jnp.int32),
            pltpu.VMEM((3 * blocks, 16, width), BF16),
            pltpu.VMEM((blocks, 16, width), BF16),
            pltpu.VMEM((nbrs * width, width), F32),
            pltpu.VMEM((nbrs * width, width), F32),
            pltpu.VMEM((2 * width, filters * width), BF16),
            pltpu.VMEM((2 * width, filters * width), BF16),
            pltpu.VMEM((blocks, (nbrs - 2) * width, filters * width), BF16),
            pltpu.VMEM((blocks, channels, filters * width), F32),
            pltpu.VMEM((filters * channels, blocks * width), BF16),
            pltpu.VMEM((blocks, channels, width), F32),
            pltpu.VMEM((blocks, channels, width), BF16),
            pltpu.VMEM((8, lanes), jnp.int32),
            pltpu.SMEM((8, lanes), jnp.int32),
            pltpu.VMEM((slots, channels, width), BF16),
            pltpu.VMEM((slots, channels, width), BF16),
            pltpu.VMEM((own * 8, width), F32),
            pltpu.VMEM((reads * width, probes), F32),
            pltpu.VMEM((tiles, reads * width, filters * probes), BF16),
            pltpu.VMEM((filters * channels, probes), BF16),
            pltpu.VMEM((channels, max(filters * probes, blocks * width)), BF16),
            pltpu.VMEM((1 + own, channels, width), F32),
            pltpu.VMEM((slots, channels, width), BF16),
            pltpu.VMEM((peers * (cap + 1), channels, width), BF16),
            pltpu.VMEM((probe_rows, channels), F32),
            pltpu.VMEM((probe_space, channels), BF16),
            pltpu.VMEM((probe_space, channels), BF16),
            pltpu.VMEM((atom_rows, channels), F32),
            pltpu.VMEM((atom_rows + atom_rows // 2, channels), BF16),
            pltpu.VMEM((atom_rows + atom_rows // 2, channels), BF16),
            dma((2, 4)),
            dma((2, 2 * (peers - 1))),
            dma((2, 2 * (peers - 1))),
            dma((2, peers - 1)),
            dma((2, 2 * (1 + chips - 1 + peers - 1))),
            dma((2, 2 * (1 + chips * peers - 1))),
            dma,
        ],
        compiler_params=pltpu.CompilerParams(
            vmem_limit_bytes=VMEM_LIMIT, collective_id=0, has_side_effects=True
        ),
        name="network_step",
    )(
        atom_nbrs.T, tile_blocks, atom_counts, atom_feat, atom_pos.transpose(1, 0, 2), probe_pos.transpose(1, 0, 2),
        probe_target, atom_filter, probe_filter, mix_weight,
        readout.reshape(1, channels),
    )
    density, grad_atom, grad_probe, grad_mix, grad_readout = pl.pallas_call(
        unpack_kernel,
        in_specs=[vmem] * 3,
        out_specs=[vmem] * 5,
        out_shape=[
            jax.ShapeDtypeStruct((tiles, probes), F32),
            jax.ShapeDtypeStruct((channels, filters * channels), F32),
            jax.ShapeDtypeStruct((channels, filters * channels), F32),
            jax.ShapeDtypeStruct((channels, channels), F32),
            jax.ShapeDtypeStruct((1, channels), F32),
        ],
        name="unpack",
    )(density, probe_sum, atom_sum)
    return density, grad_atom, grad_probe, grad_mix, grad_readout.reshape(channels)


def solution(mesh):
    return jax.shard_map(
        body,
        mesh=mesh,
        in_specs=(
            P(("space", "tile"), None, None),
            P(("space", "tile"), None, None),
            P(("space", "tile")),
            P(("space", "tile"), None),
            P(("space", "tile"), None, None),
            P(("space", "tile"), None),
            P(("space", "tile"), None),
            P(),
            P(),
            P(),
            P(),
        ),
        out_specs=(P(("space", "tile"), None), P(), P(), P(), P()),
        check_vma=False,
    )
```

```python
import functools
import math

import jax
import jax.numpy as jnp
from jax import lax
from jax.experimental import pallas as pl
from jax.experimental.pallas import tpu as pltpu
from jax.sharding import PartitionSpec as P

CUTOFF = 6.0
SPACING = 0.75
SPREAD = 0.75
LOG2E = 1.4426950408889634
MESH = pl.DeviceIdType.MESH
VMEM_LIMIT = 60 * 1024 * 1024
F32 = jnp.float32
BF16 = jnp.bfloat16
KAPPA = 2.0 * SPACING / SPREAD / SPREAD * LOG2E
BUMP = (0.9999997912905728, -0.23369419608566247, 0.01993802762546961, -0.0008456218103791793)


def silu_slope(values):
    s = jax.nn.sigmoid(values)
    return s * (1.0 + values * (1.0 - s))


def dot(a, b):
    return jnp.dot(a, b, preferred_element_type=F32)


def dot_nt(a, b):
    return lax.dot_general(a, b, (((1,), (1,)), ((), ())), preferred_element_type=F32)


def dot_tn(a, b):
    return lax.dot_general(a, b, (((0,), (0,)), ((), ())), preferred_element_type=F32)


def radial(square, factor, filters):
    middle = filters // 2
    step = SPACING / SPREAD
    edge = (CUTOFF * KAPPA) ** 2
    base = [
        math.sqrt(factor) * math.exp(-0.5 * (middle * step) ** 2) * c / edge ** (k + 1)
        for k, c in enumerate(BUMP)
    ]
    reach = square * lax.rsqrt(square)
    up = jnp.exp2(reach - (2 * middle + 1) * step * step * LOG2E)
    down = jnp.exp2((2 * middle - 1) * step * step * LOG2E - reach)
    bell = jnp.exp2(square * (-LOG2E / (SPREAD * KAPPA) ** 2) + reach * float(middle))
    wave = ((base[3] * square + base[2]) * square + base[1]) * square + base[0]
    wave = wave * jnp.maximum(edge - square, 0.0)
    values = [None] * filters
    values[middle] = bell * (wave * wave)
    for r in range(middle + 1, filters):
        k = r - middle - 1
        values[r] = values[r - 1] * (up if k == 0 else up * math.exp(-2.0 * k * step * step))
    for r in range(middle - 1, -1, -1):
        k = middle - 1 - r
        values[r] = values[r + 1] * (down if k == 0 else down * math.exp(-2.0 * k * step * step))
    return values


def thirds(values):
    out = []
    for _ in range(3):
        part = values.astype(BF16).astype(F32)
        out.append(part)
        values = values - part
    return out


def source_rows(where):
    x = [where[c : c + 1] for c in range(3)]
    norm = thirds(KAPPA**2 * (x[0] * x[0] + x[1] * x[1] + x[2] * x[2]))
    one = jnp.ones_like(x[0])
    return jnp.concatenate(x * 3 + norm + [one] * 3 + [one * 0.0], axis=0).astype(BF16)


def target_rows(where):
    y = [where[c : c + 1] for c in range(3)]
    norm = thirds(KAPPA**2 * (y[0] * y[0] + y[1] * y[1] + y[2] * y[2] + 0.01))
    y = [thirds(-2.0 * KAPPA**2 * part) for part in y]
    one = jnp.ones_like(norm[0])
    rows = [y[c][k] for k in range(3) for c in range(3)] + [one] * 3 + norm + [one * 0.0]
    return jnp.concatenate(rows, axis=0).astype(BF16)


def slot_tables(rows, me, peers, cap, blocks, reads):
    lanes = rows.shape[1]
    cols = rows.T
    row = lambda n: rows[n : n + 1, :]
    col = lambda n: cols[:, n : n + 1]
    block, owner, asker, tile, place = range(5)
    down = lax.broadcasted_iota(jnp.int32, (lanes, lanes), 0)
    along = lax.broadcasted_iota(jnp.int32, (lanes, lanes), 1)
    lane = along.astype(F32)
    yes = lambda cond: jnp.where(cond, 1.0, 0.0)
    same = yes(col(asker) == row(asker))
    equal = same * yes(col(block) == row(block))
    first_row = yes(jnp.sum(equal * yes(down < along), axis=0, keepdims=True) < 0.5)
    first_col = yes(jnp.sum(equal * yes(along < down), axis=1, keepdims=True) < 0.5)
    group = same * yes(col(owner) == row(owner))
    rank_col = jnp.sum(group * yes(row(block) < col(block)) * first_row, axis=1, keepdims=True)
    rank_row = jnp.sum(group * yes(col(block) < row(block)) * first_col, axis=0, keepdims=True)
    mine = yes(col(owner) == me) * first_col
    spot = col(block) - me * float(blocks)
    led_row = yes(jnp.sum(yes(spot == lane) * mine * yes(rank_col < 0.5), axis=0, keepdims=True) > 0.5)
    mine_row = yes(row(owner) == me) * first_row * yes(rank_row < 0.5)
    depth = down.astype(F32)
    led_col = yes(
        jnp.sum(yes(row(block) - me * float(blocks) == depth) * mine_row, axis=1, keepdims=True) > 0.5
    )
    leaders = jnp.sum(led_col, axis=0, keepdims=True)
    ahead_row = jnp.sum(led_col * yes(down < along), axis=0, keepdims=True)
    ahead_col = jnp.sum(led_row * yes(along < down), axis=1, keepdims=True)
    turn_row = led_row * ahead_row + (1.0 - led_row) * (leaders + lane[:1] - ahead_row)
    turn_col = led_col * ahead_col + (1.0 - led_col) * (leaders + depth[:, :1] - ahead_col)
    spot = jnp.sum(yes(spot == lane) * turn_row, axis=1, keepdims=True)
    put = lambda cond, value: jnp.sum(yes(cond) * value, axis=0, keepdims=True)
    asked = put(col(asker) * cap + rank_col == lane, mine * spot)
    slot = row(owner) * cap + rank_row
    arrival = put(col(asker) * blocks + spot == lane, mine * (rank_col + 1.0))
    slot_col = col(owner) * cap + rank_col
    own = yes(col(asker) == me)
    fill = put(col(tile) * (peers * cap) + slot_col == lane, own * (col(place) + 1.0))
    work = put(turn_col == lane, yes(depth[:, :1] < blocks) * depth[:, :1])
    limit = lambda value, most: jnp.clip(value, 0.0, float(most))
    rows = [
        limit(asked, blocks - 1), limit(slot, peers * cap - 1), limit(arrival, cap), limit(fill, reads),
        limit(work, blocks - 1), jnp.zeros((3, lanes), F32),
    ]
    return jnp.concatenate(rows, axis=0).astype(jnp.int32)


def within(value, most):
    return jnp.minimum(jnp.maximum(value, 0), most)


def send(source, target, send_sem, recv_sem, device):
    copy = pltpu.make_async_remote_copy(
        src_ref=source, dst_ref=target, send_sem=send_sem, recv_sem=recv_sem,
        device_id=device, device_id_type=MESH,
    )
    copy.start()
    return copy


def reduce(groups, total, sending, landing, gathered, send_sems, recv_sems, sent):
    def go(source, target, device):
        n = len(sent)
        sent.append(send(source, target, send_sems.at[n], recv_sems.at[n], device))
        return sent[-1]

    start, extent, place, bases = 0, total.shape[0], 0, []
    for size, here, others in groups:
        sending[place : place + extent, :] = total[pl.ds(start, extent), :].astype(BF16)
        part = extent // size
        copies = []
        for d, (index, device) in enumerate(others):
            source = sending.at[pl.ds(pl.multiple_of(place + index * part, 16), part)]
            copies.append(go(source, landing.at[pl.ds(place + d * part, part)], device))
        yield
        bases.append((start, extent))
        start = pl.multiple_of(start + here * part, 16)
        for copy in copies:
            copy.wait_recv()
        add = total[pl.ds(start, part), :]
        for d in range(len(others)):
            add = add + landing[place + d * part : place + (d + 1) * part, :].astype(F32)
        total[pl.ds(start, part), :] = add
        place += extent
        extent = part
    gathered[pl.ds(start, extent), :] = total[pl.ds(start, extent), :].astype(BF16)
    for n in range(len(groups) - 1, -1, -1):
        mine = gathered.at[pl.ds(start, extent)]
        copies = [go(mine, mine, device) for _, device in groups[n][2]]
        yield
        for copy in copies:
            copy.wait_recv()
        start, extent = bases[n]


def step_kernel(
    space_count, peers, cap,
    nbrs_ref, reads_ref, counts_ref, feat_ref, pos_ref, probe_ref, target_ref, atom_filter_ref, probe_filter_ref,
    mix_ref, readout_ref,
    density_ref, probe_sum_ref, atom_sum_ref,
    near_feats, far_feats, where_ref, keeps, places, region, notes_ref, notes, sources, targets, square, other_square, stage, other_stage, atom_rad, partial, sums, message, updated, table, index,
    sent, replies, read_where, probe_rad, summed, kept, grads, backs, sent_back, returned,
    probe_total, probe_sending, probe_landing, atom_total, atom_sending, atom_landing,
    near_sems, tile_sems, reply_sems, return_sems, probe_sems, atom_sems, table_sem,
):
    blocks, channels, width = feat_ref.shape
    _, tiles, probes = probe_ref.shape
    filters = atom_filter_ref.shape[1] // channels
    nbrs = nbrs_ref.shape[0]
    reads = reads_ref.shape[1]
    own = tiles * reads
    slots = peers * cap
    s, t = lax.axis_index("space"), lax.axis_index("tile")
    low, high = (s + space_count - 1) % space_count, (s + 1) % space_count
    core = s % 2
    sibling = s - core + (1 - core)
    cross = (s + 2 * core - 1 + space_count) % space_count
    chips = space_count // 2
    row = s // 2
    hops = sorted(range(1, peers), key=lambda d: -min(d, peers - d))
    tile_peers = [(t + d) % peers for d in hops]
    row_peers = [(row + d) % chips for d in range(1, chips)]
    pair_group = (2, core, [(1 - core, {"space": sibling})])
    row_group = (chips, row, [(r, {"space": r * 2 + core}) for r in row_peers])
    tile_group = (peers, t, [(p, {"tile": p}) for p in tile_peers])
    chip_list = []
    for a in range(chips):
        for b in range(peers):
            if a or b:
                r, p = (row + a) % chips, (t + b) % peers
                chip_list.append((r * peers + p, {"space": r * 2 + core, "tile": p}))
    chip_group = (chips * peers, row * peers + t, chip_list)

    barrier = pltpu.get_barrier_semaphore()
    greeted = [{"space": sibling}, {"space": cross}] + [d for _, d in chip_list]
    for device in greeted:
        pl.semaphore_signal(barrier, inc=1, device_id=device, device_id_type=MESH)
    lane = lax.broadcasted_iota(jnp.int32, (1, width), 1)
    keep = [jnp.where(lane < counts_ref[b], 1.0, 0.0) for b in range(blocks)]
    for b in range(blocks):
        keeps[b] = jnp.broadcast_to(keep[b], (8, width))
        near_feats[b] = (feat_ref[b].astype(F32) * keep[b]).astype(BF16)
    pos = [pos_ref[c].astype(F32) for c in range(3)]
    for b in range(0, blocks, 4):
        rows = [part[n : n + 1] if c < 3 else keep[n] for n in range(b, b + 4) for c, part in enumerate(pos + [keep])]
        where_ref[4 * b : 4 * b + 16, :] = jnp.concatenate(rows, axis=0).astype(BF16)
    sub = lax.broadcasted_iota(jnp.int32, notes_ref.shape, 0)
    lane = lax.broadcasted_iota(jnp.int32, notes_ref.shape, 1)
    note = jnp.zeros(notes_ref.shape, jnp.int32)
    flat = [lax.rem(reads_ref[n // reads, n % reads], peers * blocks) for n in range(own)]
    for n in range(own):
        value = jnp.where(sub == 0, flat[n], jnp.where(sub == 1, lax.div(flat[n], blocks), 0))
        value = jnp.where(sub == 2, t, jnp.where(sub == 3, n // reads, jnp.where(sub == 4, n % reads, value)))
        note = jnp.where(lane == t * own + n, value, note)
    notes_ref[...] = note
    region[pl.ds(pl.multiple_of(t * 4 * blocks, 16), 4 * blocks), :] = where_ref[...]
    notes[t] = notes_ref[...]
    pl.semaphore_wait(barrier, len(greeted))

    place_copies = [
        send(where_ref, places.at[1], near_sems.at[0, 0], near_sems.at[1, 0], {"space": low}),
        send(where_ref, places.at[0], near_sems.at[0, 1], near_sems.at[1, 1], {"space": high}),
    ]
    own_feats = near_feats.at[pl.ds(0, blocks)]
    sibling_copy = send(
        own_feats, near_feats.at[pl.ds(blocks, blocks)], near_sems.at[0, 2], near_sems.at[1, 2], {"space": sibling}
    )
    cross_copy = send(own_feats, far_feats, near_sems.at[0, 3], near_sems.at[1, 3], {"space": cross})
    tile_copies = []
    for d, p in enumerate(tile_peers):
        mine = pl.ds(pl.multiple_of(t * 4 * blocks, 16), 4 * blocks)
        tile_copies.append(
            send(notes_ref, notes.at[t], tile_sems.at[0, 2 * d], tile_sems.at[1, 2 * d], {"tile": p})
        )
        tile_copies.append(
            send(where_ref, region.at[mine], tile_sems.at[0, 2 * d + 1], tile_sems.at[1, 2 * d + 1], {"tile": p})
        )

    for b in range(blocks):
        where = where_ref[4 * b : 4 * b + 4, :].astype(F32)
        sources[blocks + b] = source_rows(where)
        targets[b] = target_rows(where)
    for copy in place_copies:
        copy.wait_recv()
    for side in range(2):
        for b in range(blocks):
            where = places[side, 4 * b : 4 * b + 4, :].astype(F32)
            sources[2 * blocks * side + b] = source_rows(where)

    order = [1 - core, 2, core] + list(range(3, nbrs))
    half = 2 * width

    def spot(b, k):
        return within(lax.rem(nbrs_ref[k, b], blocks), blocks - 1)

    def side(b, k):
        block = nbrs_ref[k, b]
        return lax.rem(lax.div(block, peers * blocks) + (space_count + 1) - s, space_count)

    factor = (nbrs * width) ** (-0.5)
    chunk = 32

    def atom_radial(b, square, stage):
        rows = [sources[within(side(b, k) * blocks + spot(b, k), 3 * blocks - 1)] for k in order]
        square[...] = dot_tn(jnp.concatenate(rows, axis=1), targets[b])
        for low in range(0, nbrs * width, chunk):
            for r, value in enumerate(radial(square[low : low + chunk, :], factor, filters)):
                at = slice(r * width, (r + 1) * width)
                if low < half:
                    stage[low : low + chunk, at] = value.astype(BF16)
                else:
                    atom_rad[b, low - half : low - half + chunk, at] = value.astype(BF16)

    def near_part(b, stage):
        feats = jnp.concatenate(
            [near_feats[blocks + spot(b, order[0])], near_feats[spot(b, order[1])]], axis=1
        )
        for r in range(0, filters, 2):
            at = slice(r * width, (r + 2) * width)
            partial[b, :, at] = dot(feats, stage[:, at])

    def two_blocks(n, carry):
        b = 2 * n
        near_part(b, stage)
        atom_radial(b + 1, other_square, other_stage)
        near_part(b + 1, other_stage)
        atom_radial(b + 2, square, stage)
        return carry

    sibling_copy.wait_recv()
    atom_radial(0, square, stage)
    lax.fori_loop(0, blocks // 2 - 1, two_blocks, 0)
    near_part(blocks - 2, stage)
    atom_radial(blocks - 1, other_square, other_stage)
    near_part(blocks - 1, other_stage)

    for copy in tile_copies:
        copy.wait_recv()
    rows = notes[0]
    for p in range(1, peers):
        rows = rows + notes[p]
    table[...] = slot_tables(rows.astype(F32), t.astype(F32), peers, cap, blocks, reads)
    to_scalars = pltpu.make_async_copy(table, index, table_sem)
    to_scalars.start()
    to_scalars.wait()
    shape = (region.shape[0], own * 8)
    lane = lax.broadcasted_iota(jnp.int32, (1, own * 8), 1)
    part = jnp.bitwise_and(lane, 7)
    want = jnp.full((1, own * 8), -8, jnp.int32)
    for n in range(own):
        want = jnp.where(jnp.logical_and(lane >= 8 * n, lane < 8 * n + 4), 4 * flat[n] + part, want)
    pick = jnp.where(lax.broadcasted_iota(jnp.int32, shape, 0) == want, 1.0, 0.0).astype(BF16)
    read_where[...] = dot_tn(pick, region[...])

    cross_copy.wait_recv()

    def atom_sums(n):
        b = within(index[4, n], blocks - 1)
        parts = [far_feats[spot(b, order[2])]]
        for k in order[3:]:
            from_far = jnp.where(side(b, k) == 2 * core, 1.0, 0.0)
            row = jnp.where(side(b, k) == 1, spot(b, k), blocks + spot(b, k))
            here = near_feats[within(row, 2 * blocks - 1)].astype(F32)
            there = far_feats[spot(b, k)].astype(F32)
            parts.append((there * from_far + here * (1.0 - from_far)).astype(BF16))
        feats = jnp.concatenate(parts, axis=1)
        at = pl.ds(pl.multiple_of(n * width, width), width)
        for r in range(0, filters, 2):
            part = dot(feats, atom_rad[b, :, r * width : (r + 2) * width])
            part = part + partial[b, :, r * width : (r + 2) * width]
            sums[r * channels : (r + 1) * channels, at] = part[:, :width].astype(BF16)
            sums[(r + 1) * channels : (r + 2) * channels, at] = part[:, width:].astype(BF16)
        return b

    def atom_layer(m, carry):
        own = [atom_sums(2 * m), atom_sums(2 * m + 1)]
        outs = dot(atom_filter_ref[...], sums[:, pl.ds(pl.multiple_of(m * 2 * width, 2 * width), 2 * width)])
        for n, b in enumerate(own):
            out = outs[:, n * width : (n + 1) * width]
            message[2 * m + n] = out
            fresh = near_feats[b].astype(F32) + out * jax.nn.sigmoid(out) * keeps[b][:1, :]
            updated[2 * m + n] = fresh.astype(BF16)
        return carry

    first = min(peers, blocks)
    first += first % 2
    reply_copies = []

    def reply(low, high):
        def fetch(p):
            for c in range(low, high):
                sent[p * cap + c] = updated[within(index[0, p * cap + c], blocks - 1)]

        for p in tile_peers:
            fetch(p)
            d = len(reply_copies)
            reply_copies.append(
                send(
                    sent.at[pl.ds(p * cap + low, high - low)], replies.at[pl.ds(t * cap + low, high - low)],
                    reply_sems.at[0, d], reply_sems.at[1, d], {"tile": p},
                )
            )
        fetch(t)

    lax.fori_loop(0, first // 2, atom_layer, 0, unroll=2)
    reply(0, 1)
    lax.fori_loop(first // 2, blocks // 2, atom_layer, 0, unroll=2)
    reply(1, cap)

    mine = pl.ds(t * cap, cap)
    replies[mine] = sent[mine]
    probe_factor = (reads * width) ** (-0.5)
    span = min(256, probes)
    for tile in range(tiles):
        target = target_rows(jnp.concatenate([probe_ref[c, tile : tile + 1, :] for c in range(3)], axis=0))
        for k in range(reads):
            low = (tile * reads + k) * 8
            partial[k, :, :probes] = dot_tn(source_rows(read_where[low : low + 8, :]), target)

        def fill(step, carry, tile=tile):
            at = pl.ds(pl.multiple_of(step * 16, 16), 16)
            k, low = lax.div(step, width // 16), pl.multiple_of(lax.rem(step, width // 16) * 16, 16)
            for p in range(0, probes, span):
                for r, value in enumerate(radial(partial[k, pl.ds(low, 16), p : p + span], probe_factor, filters)):
                    probe_rad[tile, at, r * probes + p : r * probes + p + span] = value.astype(BF16)
            return carry

        lax.fori_loop(0, reads * width // 16, fill, 0, unroll=4)
    for copy in reply_copies:
        copy.wait_recv()

    readout = jnp.broadcast_to(readout_ref[...], (8, channels)).T[:, :1]
    backs[0] = jnp.zeros_like(backs[0])
    grad_readout = None
    for tile in range(tiles):
        across = slice(tile * probes, (tile + 1) * probes)
        feats = jnp.concatenate(
            [replies[within(index[1, (t * tiles + tile) * reads + k], slots - 1)] for k in range(reads)], axis=1
        )

        def forward(r, carry, tile=tile, feats=feats, across=across):
            at = pl.ds(pl.multiple_of(r * probes, probes), probes)
            part = dot(feats, probe_rad[tile, :, at])
            summed[pl.ds(pl.multiple_of(r * channels, channels), channels), across] = part.astype(BF16)
            return carry

        lax.fori_loop(0, filters, forward, 0, unroll=True)
        hidden = dot(probe_filter_ref[...], summed[:, across])
        gate = jax.nn.sigmoid(hidden)
        squashed = (hidden * gate).astype(BF16)
        mixed = dot(mix_ref[...], squashed)
        mixed_gate = jax.nn.sigmoid(mixed)
        outer = mixed * mixed_gate
        density = jnp.sum(readout * outer, axis=0, keepdims=True)
        density_ref[tile : tile + 1, :] = density
        misfit = (density - target_ref[tile : tile + 1, :]) / probes
        part = jnp.sum(outer * misfit, axis=1, keepdims=True)
        part = jnp.broadcast_to(part, (channels, channels)).T[:16, :]
        grad_readout = part if grad_readout is None else grad_readout + part
        grad_mixed = (readout * misfit * (mixed_gate * (1.0 + mixed * (1.0 - mixed_gate)))).astype(BF16)
        grad_squashed = dot_tn(mix_ref[...], grad_mixed)
        grad_hidden = (grad_squashed * (gate * (1.0 + hidden * (1.0 - gate)))).astype(BF16)
        for n, value in enumerate((grad_hidden, grad_mixed, squashed)):
            kept[n, :, across] = value
        for r in range(filters):
            piece = dot_tn(probe_filter_ref[:, r * channels : (r + 1) * channels], grad_hidden)
            grads[:, r * probes : (r + 1) * probes] = piece.astype(BF16)
        for k in range(0, reads, 2):
            back = dot_nt(grads[...], probe_rad[tile, k * width : (k + 2) * width, :])
            for n in range(2):
                backs[1 + tile * reads + k + n] = back[:, n * width : (n + 1) * width]
    def fetch_back(p):
        for c in range(cap):
            slot = p * cap + c
            total = backs[within(index[3, slot], reads)]
            for tile in range(1, tiles):
                place = within(index[3, tile * slots + slot], reads)
                total = total + backs[jnp.where(place > 0, place + tile * reads, 0)]
            sent_back[slot] = total.astype(BF16)

    step = cap + 1
    landing = pl.ds(t * step + 1, cap)
    return_copies = []

    def give_back(count):
        for p in tile_peers[len(return_copies) :][:count]:
            fetch_back(p)
            d = len(return_copies)
            return_copies.append(
                send(
                    sent_back.at[pl.ds(p * cap, cap)], returned.at[landing],
                    return_sems.at[0, d], return_sems.at[1, d], {"tile": p},
                )
            )

    give_back(peers // 2 - 1)
    fetch_back(t)
    for p in range(peers):
        returned[p * step] = jnp.zeros((channels, width), BF16)
    returned[landing] = sent_back[mine]
    base = filters * channels
    for r in range(0, filters, 2):
        part = dot_nt(kept[0], summed[r * channels : (r + 2) * channels, :])
        probe_total[r * channels : (r + 1) * channels, :] = part[:, :channels]
        probe_total[(r + 1) * channels : (r + 2) * channels, :] = part[:, channels:]
    probe_total[base : base + channels, :] = dot_nt(kept[1], kept[2])
    probe_total[base + channels : base + channels + 16, :] = grad_readout
    spare = probe_total.shape[0] - base - channels - 16
    if spare:
        probe_total[base + channels + 16 :, :] = jnp.zeros((spare, channels), F32)

    probe_copies, atom_copies = [], []
    probe_steps = reduce(
        [pair_group, row_group, tile_group], probe_total, probe_sending, probe_landing, probe_sum_ref,
        probe_sems.at[0], probe_sems.at[1], probe_copies,
    )
    atom_steps = reduce(
        [pair_group, chip_group], atom_total, atom_sending, atom_landing, atom_sum_ref,
        atom_sems.at[0], atom_sems.at[1], atom_copies,
    )
    next(probe_steps)
    give_back(peers // 4)
    next(probe_steps)
    give_back(peers)
    for copy in return_copies:
        copy.wait_recv()

    def atom_grad(b, carry):
        total = None
        for p in range(peers):
            part = returned[p * step + within(index[2, p * blocks + b], cap)].astype(F32)
            total = part if total is None else total + part
        grad = total * keeps[within(index[4, b], blocks - 1)][:1, :] * silu_slope(message[b])
        grads[:, pl.ds(pl.multiple_of(b * width, width), width)] = grad.astype(BF16)
        return carry

    lax.fori_loop(0, blocks, atom_grad, 0, unroll=4)
    for r in range(0, filters, 2):
        part = dot_nt(grads[:, : blocks * width], sums[r * channels : (r + 2) * channels, :])
        for n in range(2):
            at = slice((r + n) * channels, (r + n + 1) * channels)
            atom_total[at, :] = part[:, n * channels : (n + 1) * channels]
    spare = atom_total.shape[0] - base
    if spare:
        atom_total[base:, :] = jnp.zeros((spare, channels), F32)
    turn = [atom_steps, probe_steps]
    while turn:
        turn = [steps for steps in turn if next(steps, 0) is None]
    every = place_copies + [sibling_copy, cross_copy] + tile_copies + reply_copies + return_copies + probe_copies + atom_copies
    for copy in every:
        copy.wait_send()


def unpack_kernel(density_ref, probe_ref, atom_ref, out_ref, grad_atom_ref, grad_probe_ref, grad_mix_ref, readout_ref):
    channels = grad_mix_ref.shape[0]
    filters = grad_atom_ref.shape[1] // channels
    out_ref[...] = density_ref[...]
    for r in range(filters):
        at = slice(r * channels, (r + 1) * channels)
        grad_atom_ref[:, at] = atom_ref[at, :].astype(F32)
        grad_probe_ref[:, at] = probe_ref[at, :].astype(F32)
    base = filters * channels
    grad_mix_ref[...] = probe_ref[base : base + channels, :].astype(F32)
    readout_ref[...] = probe_ref[base + channels : base + channels + 16, :].astype(F32)[:1]


def body(
    atom_feat, atom_pos, atom_counts, atom_nbrs, probe_pos, probe_target, tile_blocks,
    atom_filter, probe_filter, mix_weight, readout,
):
    blocks, channels, width = atom_feat.shape
    tiles, reads = tile_blocks.shape
    probes = probe_pos.shape[2]
    filters = atom_filter.shape[1] // channels
    nbrs = atom_nbrs.shape[1]
    peers = lax.axis_size("tile")
    space_count = lax.axis_size("space")
    devices = peers * space_count
    cap = max(2, 2 * reads * tiles // peers)
    slots = peers * cap
    own = tiles * reads
    lanes = max(peers * own, peers * blocks, tiles * slots)
    unit = 16 * devices
    atom_rows = -(-filters * channels // unit) * unit
    probe_rows = -(-(filters * channels + channels + 16) // unit) * unit
    vmem = pl.BlockSpec(memory_space=pltpu.VMEM)
    smem = pl.BlockSpec(memory_space=pltpu.SMEM)
    dma = pltpu.SemaphoreType.DMA
    chips = space_count // 2
    probe_space = probe_rows + probe_rows // 2 + probe_rows // (2 * chips)
    density, probe_sum, atom_sum = pl.pallas_call(
        functools.partial(step_kernel, space_count, peers, cap),
        in_specs=[smem] * 3 + [vmem] * 8,
        out_specs=[vmem] * 3,
        out_shape=[
            jax.ShapeDtypeStruct((tiles, probes), F32),
            jax.ShapeDtypeStruct((probe_rows, channels), BF16),
            jax.ShapeDtypeStruct((atom_rows, channels), BF16),
        ],
        scratch_shapes=[
            pltpu.VMEM((2 * blocks, channels, width), BF16),
            pltpu.VMEM((blocks, channels, width), BF16),
            pltpu.VMEM((4 * blocks, width), BF16),
            pltpu.VMEM((blocks, 8, width), F32),
            pltpu.VMEM((2, 4 * blocks, width), BF16),
            pltpu.VMEM((peers * 4 * blocks, width), BF16),
            pltpu.VMEM((8, lanes), jnp.int32),
            pltpu.VMEM((peers, 8, lanes), jnp.int32),
            pltpu.VMEM((3 * blocks, 16, width), BF16),
            pltpu.VMEM((blocks, 16, width), BF16),
            pltpu.VMEM((nbrs * width, width), F32),
            pltpu.VMEM((nbrs * width, width), F32),
            pltpu.VMEM((2 * width, filters * width), BF16),
            pltpu.VMEM((2 * width, filters * width), BF16),
            pltpu.VMEM((blocks, (nbrs - 2) * width, filters * width), BF16),
            pltpu.VMEM((blocks, channels, filters * width), F32),
            pltpu.VMEM((filters * channels, blocks * width), BF16),
            pltpu.VMEM((blocks, channels, width), F32),
            pltpu.VMEM((blocks, channels, width), BF16),
            pltpu.VMEM((8, lanes), jnp.int32),
            pltpu.SMEM((8, lanes), jnp.int32),
            pltpu.VMEM((slots, channels, width), BF16),
            pltpu.VMEM((slots, channels, width), BF16),
            pltpu.VMEM((own * 8, width), F32),
            pltpu.VMEM((tiles, reads * width, filters * probes), BF16),
            pltpu.VMEM((filters * channels, tiles * probes), BF16),
            pltpu.VMEM((3, channels, tiles * probes), BF16),
            pltpu.VMEM((channels, max(filters * probes, blocks * width)), BF16),
            pltpu.VMEM((1 + own, channels, width), F32),
            pltpu.VMEM((slots, channels, width), BF16),
            pltpu.VMEM((peers * (cap + 1), channels, width), BF16),
            pltpu.VMEM((probe_rows, channels), F32),
            pltpu.VMEM((probe_space, channels), BF16),
            pltpu.VMEM((probe_space, channels), BF16),
            pltpu.VMEM((atom_rows, channels), F32),
            pltpu.VMEM((atom_rows + atom_rows // 2, channels), BF16),
            pltpu.VMEM((atom_rows + atom_rows // 2, channels), BF16),
            dma((2, 4)),
            dma((2, 2 * (peers - 1))),
            dma((2, 2 * (peers - 1))),
            dma((2, peers - 1)),
            dma((2, 2 * (1 + chips - 1 + peers - 1))),
            dma((2, 2 * (1 + chips * peers - 1))),
            dma,
        ],
        compiler_params=pltpu.CompilerParams(
            vmem_limit_bytes=VMEM_LIMIT, collective_id=0, has_side_effects=True
        ),
        name="network_step",
    )(
        atom_nbrs.T, tile_blocks, atom_counts, atom_feat, atom_pos.transpose(1, 0, 2), probe_pos.transpose(1, 0, 2),
        probe_target, atom_filter, probe_filter, mix_weight,
        readout.reshape(1, channels),
    )
    density, grad_atom, grad_probe, grad_mix, grad_readout = pl.pallas_call(
        unpack_kernel,
        in_specs=[vmem] * 3,
        out_specs=[vmem] * 5,
        out_shape=[
            jax.ShapeDtypeStruct((tiles, probes), F32),
            jax.ShapeDtypeStruct((channels, filters * channels), F32),
            jax.ShapeDtypeStruct((channels, filters * channels), F32),
            jax.ShapeDtypeStruct((channels, channels), F32),
            jax.ShapeDtypeStruct((1, channels), F32),
        ],
        name="unpack",
    )(density, probe_sum, atom_sum)
    return density, grad_atom, grad_probe, grad_mix, grad_readout.reshape(channels)


def solution(mesh):
    return jax.shard_map(
        body,
        mesh=mesh,
        in_specs=(
            P(("space", "tile"), None, None),
            P(("space", "tile"), None, None),
            P(("space", "tile")),
            P(("space", "tile"), None),
            P(("space", "tile"), None, None),
            P(("space", "tile"), None),
            P(("space", "tile"), None),
            P(),
            P(),
            P(),
            P(),
        ),
        out_specs=(P(("space", "tile"), None), P(), P(), P(), P()),
        check_vma=False,
    )
```
